128 devices in a mesh: dp: 8 (over z, core), expert: 16 (over y, x).
Axes of the slice: x: 4, y: 4, z: 4, core: 2. Of those that a mesh axis runs over, the one named last changes fastest.
Arguments:
- tokens_in: bfloat16 [16384, 4096], P(('dp', 'expert')), may hold values from -6 to 6
- out_grad: bfloat16 [16384, 4096], P(('dp', 'expert')), may hold values from -3 to 3
- expert_ids: int32 [16384, 2], P(('dp', 'expert')), may hold values from 0 to 15, all different within a row; in each aligned block of 128 rows (0 to 127, 128 to 255, ...) at most 32 rows name the same one
- gate_probs: bfloat16 [16384, 2], P(('dp', 'expert')), may hold values from 0.099609375 to 1
- gate_up: bfloat16 [4096, 2, 16, 768], P(None, None, 'expert'), may hold values from -0.09375 to 0.09375
- down_proj: bfloat16 [4096, 16, 768], P(None, 'expert'), may hold values from -0.21875 to 0.21875
Outputs:
- input_grad: bfloat16 [16384, 4096], P(('dp', 'expert'))
- gate_grad: bfloat16 [16384, 2], P(('dp', 'expert'))
- gate_up_grad: bfloat16 [4096, 2, 16, 768], P('dp', None, 'expert')
- down_grad: bfloat16 [4096, 16, 768], P('dp', 'expert')
The draws below stay inside these ranges and needn't reach their ends.
Inputs may be any that keep to these rules, and one draw needn't show every extreme that they name: `expert_ids`: each row names 2 different experts. The rows of one device name no expert more than 32 times, and in every draw some device's rows name some expert exactly 32 times.
All inputs are finite; a program needn't handle non-finite values.
Results may differ from the reference program's by a relative error of at most 0.017.
Values may be sent and summed in bfloat16 or wider, within the bound.
No kernel may reach another device: no remote copies, remote signals or barrier semaphores. Data moves between devices by JAX's collectives and lax.ppermute only.
A program may use at most 192 MiB of HBM per device.

```python
import math
import jax
import jax.numpy as jnp
import numpy as np
from jax import lax

D = 4096
FF = 768
TOP_WIN = 2
TOK_DEV = 128
EXPERTS = 16
CAP = 32
TOKENS = 16384
N_DP = 8
N_EXPERT = 16


def shard_levels(stream_key, extent, pieces, low, largest):
    def one(dim, blocks):
        heights = jax.random.uniform(jax.random.fold_in(jax.random.fold_in(stream_key, 6), dim), (blocks,), jnp.float32, low / len(pieces), largest / len(pieces))
        return jnp.repeat(jnp.exp(heights), extent[dim] // blocks).reshape((-1,) + (1,) * (len(extent) - dim - 1))

    loudness = one(*pieces[0])
    for cut in pieces[1:]:
        loudness = loudness * one(*cut)
    return loudness


def routed_block(stream_key, own, number, rows, amount, top, most, slope):
    ranking = jax.random.permutation(stream_key, amount)
    crowded, common = shares(amount, rows * top, most, slope, True), shares(amount, rows * top, most, slope, False)
    places = jnp.arange(amount)

    def named(tallies, offset_by):
        used = int((tallies > 0).sum())
        fixed = max(1, used // 4)
        moved = fixed + (places - fixed + offset_by * (used - fixed)) % max(1, amount - fixed)
        return jnp.zeros((amount,), jnp.int32).at[ranking[jnp.where(places < fixed, places, moved)]].set(jnp.asarray(tallies, jnp.int32))

    tallies = jnp.where(number % 4 == 0, named(crowded, number // 4), named(common, number - number // 4 - 1))
    mixed = jax.random.permutation(jax.random.fold_in(own, 3), amount)
    giver, sink = mixed[0:amount // 2 * 2:2], mixed[1:amount // 2 * 2:2]
    margin = jnp.minimum(tallies[giver] - 1, most - tallies[sink]) // 2
    margin = jnp.where((giver == ranking[0]) | (sink == ranking[0]) | (tallies[sink] == 0), 0, jnp.maximum(margin, 0))
    moved = jax.random.randint(jax.random.fold_in(own, 4), (amount // 2,), 0, 1 << 20) % (margin + 1)
    tallies = tallies.at[giver].add(-moved).at[sink].add(moved)
    items = jnp.searchsorted(jnp.cumsum(tallies), jnp.arange(rows * top), side="right").astype(jnp.int32)
    grid = items.reshape(top, rows).T
    grid = grid[jax.random.permutation(jax.random.fold_in(own, 1), rows)]
    offset_by = jax.random.randint(jax.random.fold_in(own, 2), (rows, 1), 0, top)
    return jnp.take_along_axis(grid, (jnp.arange(top)[None, :] + offset_by) % top, axis=1)


def shares(number_of, total, reach, slope, full):
    loads = [(1 << 20) // math.isqrt(rank ** slope) + 1 for rank in range(1, number_of + 1)]
    largest = reach if full else min(reach, max(-(-total // number_of), total * loads[0] // sum(loads)))
    least = 1 if total - largest >= number_of - 1 else 0
    counts, surplus = [largest] + [least] * (number_of - 1), total - largest - least * (number_of - 1)
    while surplus > 0:
        candidates = [i for i in range(1, number_of) if counts[i] < largest] or [i for i in range(1, number_of) if counts[i] < reach]
        whole, budget = sum([loads[i] for i in candidates]), surplus
        for i in candidates:
            addition = min(reach - counts[i], max(1, budget * loads[i] // whole), surplus)
            counts[i] = counts[i] + addition
            surplus = surplus - addition
    return np.array(counts)


def scatter_about(rng, shape, scale, bound, split=(), kind=jnp.bfloat16):
    gain = shard_levels(rng, shape, split, -0.22, 0.18) if split else 1.0
    values = jax.random.normal(rng, shape, jnp.float32) * scale * gain
    return jnp.minimum(jnp.maximum(values, -bound), bound).astype(kind)


def setup_inputs(seed: int = 0) -> dict:
    keys = jax.random.split(jax.random.key(seed), 7)
    tokens_in = scatter_about(keys[0], (TOKENS, D), 1.0, 6.0, ((0, 128),))
    out_grad = scatter_about(keys[1], (TOKENS, D), 0.5, 3.0, ((0, 128),))
    expert_ids_keys = jax.random.split(jax.random.fold_in(keys[2], 1), TOKENS // TOK_DEV)
    expert_ids_turns = jax.random.permutation(jax.random.fold_in(keys[2], 3), TOKENS // TOK_DEV)
    expert_ids = jax.vmap(lambda own, number: routed_block(jax.random.fold_in(keys[2], 2), own, number, TOK_DEV, EXPERTS, TOP_WIN, CAP, 2))(expert_ids_keys, expert_ids_turns).reshape((TOKENS, TOP_WIN))
    gate_probs = jnp.clip(0.099609375 + 0.9003906 * jax.random.uniform(keys[3], (TOKENS, TOP_WIN), jnp.float32) ** shard_levels(keys[3], (TOKENS, TOP_WIN), ((0, 128),), -0.2, 0.2), 0.099609375, 1.0).astype(jnp.bfloat16)
    gate_up = scatter_about(keys[4], (D, 2, EXPERTS, FF), D ** -0.5, 0.09375, ((2, 16),))
    down_proj = scatter_about(keys[5], (D, EXPERTS, FF), FF ** -0.5, 0.21875, ((1, 16),))
    return {"tokens_in": tokens_in, "out_grad": out_grad, "expert_ids": expert_ids, "gate_probs": gate_probs, "gate_up": gate_up, "down_proj": down_proj}


def expert_rows(rows_in, grads_in, gates_in, gate_w, up_w, down_w):
    pre_gate = jnp.dot(rows_in, gate_w, preferred_element_type=jnp.float32)
    pre_up = jnp.dot(rows_in, up_w, preferred_element_type=jnp.float32)
    sigmoid_gate = jax.nn.sigmoid(pre_gate)
    activated = pre_gate * sigmoid_gate
    product = (activated * pre_up).astype(jnp.bfloat16)
    output_rows = jnp.dot(product, down_w.T, preferred_element_type=jnp.float32)
    gate_rows = jnp.sum(grads_in.astype(jnp.float32) * output_rows, axis=-1).astype(jnp.bfloat16)
    scaled = (gates_in.astype(jnp.float32)[:, None] * grads_in.astype(jnp.float32)).astype(jnp.bfloat16)
    act_grad = jnp.dot(scaled, down_w, preferred_element_type=jnp.float32)
    gate_row_grad = (act_grad * pre_up * sigmoid_gate * (1.0 + pre_gate * (1.0 - sigmoid_gate))).astype(jnp.bfloat16)
    up_row_grad = (act_grad * activated).astype(jnp.bfloat16)
    input_rows = (jnp.dot(gate_row_grad, gate_w.T, preferred_element_type=jnp.float32)
                  + jnp.dot(up_row_grad, up_w.T, preferred_element_type=jnp.float32)).astype(jnp.bfloat16)
    return gate_rows, scaled, product, gate_row_grad, up_row_grad, input_rows


def rounded_sum(partial_value):
    rounded = lax.optimization_barrier(partial_value.astype(jnp.bfloat16))
    return jnp.sum(rounded.astype(jnp.float32), axis=0).astype(jnp.bfloat16)


def reference(tokens_in, out_grad, expert_ids, gate_probs, gate_up, down_proj):
    devices = N_DP * N_EXPERT
    assign = TOK_DEV * TOP_WIN
    total = TOKENS * TOP_WIN
    width = tokens_in.shape[1]
    flat_ids = expert_ids.reshape(devices, assign).astype(jnp.int32)
    onehot = (flat_ids[:, :, None] == jnp.arange(EXPERTS, dtype=jnp.int32)[None, None, :]).astype(jnp.int32)
    placed = jnp.sum((jnp.cumsum(onehot, axis=1) - onehot) * onehot, axis=2).astype(jnp.int32)
    device_ids = jnp.broadcast_to(jnp.arange(devices, dtype=jnp.int32)[:, None], (devices, assign))
    global_ids = (device_ids * assign + jnp.arange(assign, dtype=jnp.int32)[None, :]).astype(jnp.int32)
    table = jnp.full((devices, EXPERTS, CAP), total, jnp.int32).at[device_ids, flat_ids, placed].set(global_ids)
    table = table.reshape(N_DP, N_EXPERT, EXPERTS, CAP)
    tokens_pad = jnp.concatenate([tokens_in, jnp.zeros((1, width), jnp.bfloat16)], axis=0)
    grads_pad = jnp.concatenate([out_grad, jnp.zeros((1, width), jnp.bfloat16)], axis=0)
    gates_pad = jnp.concatenate([gate_probs.reshape(total), jnp.zeros((1,), jnp.bfloat16)], axis=0)
    gate_all = gate_up[:, 0]
    up_all = gate_up[:, 1]

    def per_expert(carry, expert):
        input_acc, gate_acc = carry
        picked = lax.dynamic_index_in_dim(table, expert, axis=2, keepdims=False).reshape(N_DP * N_EXPERT * CAP).astype(jnp.int32)
        token_rows = (picked // TOP_WIN).astype(jnp.int32)
        rows_in = tokens_pad[token_rows]
        grads_in = grads_pad[token_rows]
        gates_in = gates_pad[picked]
        gate_w = lax.dynamic_index_in_dim(gate_all, expert, axis=1, keepdims=False)
        up_w = lax.dynamic_index_in_dim(up_all, expert, axis=1, keepdims=False)
        down_w = lax.dynamic_index_in_dim(down_proj, expert, axis=1, keepdims=False)
        gate_rows, scaled, product, gate_row_grad, up_row_grad, input_rows = expert_rows(
            rows_in, grads_in, gates_in, gate_w, up_w, down_w)
        input_acc = input_acc.at[token_rows].add(input_rows.astype(jnp.float32))
        gate_acc = gate_acc.at[picked].set(gate_rows)
        rows_wide = rows_in.reshape(N_DP, -1, width).astype(jnp.float32)
        scaled_wide = scaled.reshape(N_DP, -1, width).astype(jnp.float32)
        gate_part = jnp.einsum('prd,prf->pdf', rows_wide, gate_row_grad.reshape(N_DP, -1, FF).astype(jnp.float32))
        up_part = jnp.einsum('prd,prf->pdf', rows_wide, up_row_grad.reshape(N_DP, -1, FF).astype(jnp.float32))
        down_part = jnp.einsum('prd,prf->pdf', scaled_wide, product.reshape(N_DP, -1, FF).astype(jnp.float32))
        return (input_acc, gate_acc), (rounded_sum(gate_part), rounded_sum(up_part), rounded_sum(down_part))

    start = (jnp.zeros((TOKENS + 1, width), jnp.float32), jnp.zeros((total + 1,), jnp.bfloat16))
    (input_acc, gate_acc), (grads_gate, grads_up, grads_down) = lax.scan(
        per_expert, start, jnp.arange(EXPERTS, dtype=jnp.int32))
    input_grad = input_acc[:TOKENS].astype(jnp.bfloat16)
    gate_grad = gate_acc[:total].reshape(TOKENS, TOP_WIN)
    gate_up_grad = jnp.stack([grads_gate, grads_up], axis=0).transpose(2, 0, 1, 3)
    down_grad = grads_down.transpose(1, 0, 2)
    return input_grad, gate_grad, gate_up_grad, down_grad
```

```python
import functools

import jax
import jax.numpy as jnp
from jax import lax
from jax.experimental import pallas as pl
from jax.experimental.pallas import tpu as pltpu
from jax.sharding import PartitionSpec as P

BF = jnp.bfloat16
F32 = jnp.float32
SLICE = 512
PART_A = 384
PART_B = SLICE - PART_A
GROUP = SLICE + PART_A
SLICES = 8
CAP = 32
LANES = 128
VMEM_LIMIT = 48 * 1024 * 1024


def params(**extra):
    return pltpu.CompilerParams(vmem_limit_bytes=VMEM_LIMIT, **extra)


def dot_nn(a, b):
    return lax.dot_general(a, b, (((1,), (0,)), ((), ())), preferred_element_type=F32)


def dot_nt(a, b):
    return lax.dot_general(a, b, (((1,), (1,)), ((), ())), preferred_element_type=F32)


def dot_tn(a, b):
    return lax.dot_general(a, b, (((0,), (0,)), ((), ())), preferred_element_type=F32)


def pack_kernel(ids_ref, gates_ref, tok_ref, dy_ref, first_ref, second_ref, hot_ref, *, step_experts):
    tokens = ids_ref.shape[1]
    base = pl.program_id(0) * step_experts
    expert = lax.broadcasted_iota(jnp.int32, (8, tokens), 0) + base
    zero = jnp.zeros((8, tokens), F32)
    is_0 = ids_ref[0:1, :] == expert
    is_1 = ids_ref[1:2, :] == expert
    named = is_0 | is_1
    member = jnp.where(named, 1.0, 0.0).astype(BF)
    row = lax.broadcasted_iota(jnp.int32, (tokens, tokens), 0)
    col = lax.broadcasted_iota(jnp.int32, (tokens, tokens), 1)
    earlier = jnp.where(row < col, 1.0, 0.0).astype(BF)
    place = jnp.where(named, dot_nn(member, earlier), -1.0)
    gates = gates_ref[...].astype(F32)
    weight = jnp.where(is_0, gates[0:1, :], zero) + jnp.where(is_1, gates[1:2, :], zero)
    rows = step_experts * CAP
    place_all = jnp.broadcast_to(place[:step_experts, None, :], (step_experts, CAP, tokens)).reshape(rows, tokens)
    weight_all = jnp.broadcast_to(weight[:step_experts, None, :], (step_experts, CAP, tokens)).reshape(rows, tokens)
    slot = (lax.broadcasted_iota(jnp.int32, (rows, tokens), 0) % CAP).astype(F32)
    hot = jnp.where(place_all == slot, 1.0, 0.0)
    slot_gate = jnp.sum(hot * weight_all, axis=1, keepdims=True)
    first_ref[:, SLICES * GROUP :] = jnp.broadcast_to(slot_gate, (rows, LANES)).astype(BF)
    hot = hot.astype(BF)
    hot_ref[...] = hot
    for q in range(SLICES):
        cols = slice(q * SLICE, (q + 1) * SLICE)
        first_ref[:, q * GROUP : q * GROUP + SLICE] = dot_nn(hot, tok_ref[:, cols]).astype(BF)
        grads = dot_nn(hot, dy_ref[:, cols]).astype(BF)
        first_ref[:, q * GROUP + SLICE : (q + 1) * GROUP] = grads[:, :PART_A]
        second_ref[:, q * PART_B : (q + 1) * PART_B] = grads[:, PART_A:]


def pack(ids, gates, tokens_in, out_grad, slots):
    steps = 4
    tok_dev, width = tokens_in.shape
    rows = slots // steps
    wide = SLICES * GROUP + LANES
    whole = lambda shape: pl.BlockSpec(shape, lambda i: (0, 0))
    return pl.pallas_call(
        functools.partial(pack_kernel, step_experts=rows // CAP),
        grid=(steps,),
        in_specs=[whole((2, tok_dev)), whole((2, tok_dev)), whole((tok_dev, width)), whole((tok_dev, width))],
        out_specs=[
            pl.BlockSpec((rows, wide), lambda i: (i, 0)),
            pl.BlockSpec((rows, SLICES * PART_B), lambda i: (i, 0)),
            pl.BlockSpec((rows, tok_dev), lambda i: (i, 0)),
        ],
        out_shape=[
            jax.ShapeDtypeStruct((slots, wide), BF),
            jax.ShapeDtypeStruct((slots, SLICES * PART_B), BF),
            jax.ShapeDtypeStruct((slots, tok_dev), BF),
        ],
        compiler_params=params(),
        name="pack",
    )(ids, gates, tokens_in, out_grad)


def pick_kernel(index_ref, src_ref, out_ref):
    del index_ref
    out_ref[...] = src_ref[...]


def pick(src, index, width):
    rows = src.shape[0]
    return pl.pallas_call(
        pick_kernel,
        grid_spec=pltpu.PrefetchScalarGridSpec(
            num_scalar_prefetch=1,
            grid=(4,),
            in_specs=[pl.BlockSpec((rows, width), lambda i, index: (0, index[i]))],
            out_specs=pl.BlockSpec((rows, width), lambda i, index: (0, i)),
        ),
        out_shape=jax.ShapeDtypeStruct((rows, 4 * width), BF),
        compiler_params=params(),
        name="pick",
    )(index, src)


def pre_kernel(rows_ref, gate_ref, wg_ref, wu_ref, wd_ref, u_ref, c1_ref, c2_ref, p_ref, gp_ref, pg_acc, pu_acc, *, per):
    step = pl.program_id(0)

    @pl.when(step == 0)
    def _():
        pg_acc[...] = jnp.zeros_like(pg_acc)
        pu_acc[...] = jnp.zeros_like(pu_acc)
        u_ref[...] = jnp.zeros_like(u_ref)

    x = jnp.concatenate([rows_ref[:, k * GROUP : k * GROUP + SLICE] for k in range(per)], axis=1)
    pg_acc[...] += dot_nn(x, wg_ref[...])
    pu_acc[...] += dot_nn(x, wu_ref[...])
    dy = jnp.concatenate([rows_ref[:, k * GROUP + SLICE : (k + 1) * GROUP] for k in range(per)], axis=1)
    wd = jnp.concatenate([wd_ref[k * SLICE : k * SLICE + PART_A, :] for k in range(per)], axis=0)
    u_ref[...] += dot_nn(dy, wd)

    @pl.when(step == pl.num_programs(0) - 1)
    def _():
        chunk = 32

        def one(i, carry):
            at = pl.ds(pl.multiple_of(i * chunk, chunk), chunk)
            pg = pg_acc[at, :]
            pu = pu_acc[at, :]
            g = gate_ref[at, :].astype(F32)[:, :1]
            s = jax.nn.sigmoid(pg)
            a = pg * s
            product = a * pu
            p_ref[at, :] = product.astype(BF)
            gp_ref[at, :] = (g * product).astype(BF)
            c1_ref[at, :] = g * (pu * s * (1.0 + pg * (1.0 - s)))
            c2_ref[at, :] = g * a
            return carry

        lax.fori_loop(0, pg_acc.shape[0] // chunk, one, 0)


def pre(first, wg, wu, wd):
    slots = first.shape[0]
    ff = wd.shape[1]
    per = 2
    weights = pl.BlockSpec((per * SLICE, ff), lambda q: (q, 0))
    whole = pl.BlockSpec((slots, ff), lambda q: (0, 0))
    return pl.pallas_call(
        functools.partial(pre_kernel, per=per),
        grid=(SLICES // per,),
        in_specs=[
            pl.BlockSpec((slots, per * GROUP), lambda q: (0, q)),
            pl.BlockSpec((slots, LANES), lambda q: (0, SLICES * GROUP // LANES)),
            weights,
            weights,
            weights,
        ],
        out_specs=[whole] * 5,
        out_shape=[
            jax.ShapeDtypeStruct((slots, ff), F32),
            jax.ShapeDtypeStruct((slots, ff), F32),
            jax.ShapeDtypeStruct((slots, ff), F32),
            jax.ShapeDtypeStruct((slots, ff), BF),
            jax.ShapeDtypeStruct((slots, ff), BF),
        ],
        scratch_shapes=[pltpu.VMEM((slots, ff), F32)] * 2,
        compiler_params=params(),
        name="pre",
    )(first, first, wg, wu, wd)


def hidden_kernel(dy_ref, wd_ref, u_ref, c1_ref, c2_ref, p_ref, h_ref, gate_ref, u_acc, gate_acc):
    step = pl.program_id(0)
    u_acc[...] = u_ref[...] + dot_nn(dy_ref[...], wd_ref[...])

    @pl.when(step == 0)
    def _():
        gate_acc[...] = jnp.zeros_like(gate_acc)

    chunk = 64

    def one(i, carry):
        at = pl.ds(pl.multiple_of(i * chunk, chunk), chunk)
        u = u_acc[at, :]
        h_ref[0, at, :] = (u * c1_ref[at, :]).astype(BF)
        h_ref[1, at, :] = (u * c2_ref[at, :]).astype(BF)
        both = u * p_ref[at, :].astype(F32)
        folded = both[:, :LANES]
        for k in range(1, both.shape[1] // LANES):
            folded += both[:, k * LANES : (k + 1) * LANES]
        gate_acc[at, :] += folded
        return carry

    lax.fori_loop(0, u_acc.shape[0] // chunk, one, 0)

    @pl.when(step == pl.num_programs(0) - 1)
    def _():
        total = jnp.sum(gate_acc[...], axis=1, keepdims=True)
        gate_ref[...] = jnp.broadcast_to(total, gate_ref.shape).astype(BF)


def hidden(second, wd_b, u_a, c1, c2, p):
    slots, ff = p.shape
    blk = 256
    col = pl.BlockSpec((slots, blk), lambda j: (0, j))
    depth = second.shape[1]
    return pl.pallas_call(
        hidden_kernel,
        grid=(ff // blk,),
        in_specs=[
            pl.BlockSpec((slots, depth), lambda j: (0, 0)),
            pl.BlockSpec((depth, blk), lambda j: (0, j)),
            col,
            col,
            col,
            col,
        ],
        out_specs=[pl.BlockSpec((2, slots, blk), lambda j: (0, 0, j)), pl.BlockSpec((slots, LANES), lambda j: (0, 0))],
        out_shape=[jax.ShapeDtypeStruct((2, slots, ff), BF), jax.ShapeDtypeStruct((slots, LANES), BF)],
        scratch_shapes=[pltpu.VMEM((slots, blk), F32), pltpu.VMEM((slots, LANES), F32)],
        compiler_params=params(),
        name="hidden",
    )(second, wd_b, u_a, c1, c2, p)


def input_kernel(h_ref, wg_ref, wu_ref, gate_ref, out_ref):
    out_ref[...] = (dot_nt(h_ref[0], wg_ref[...]) + dot_nt(h_ref[1], wu_ref[...])).astype(BF)

    @pl.when(pl.program_id(0) == pl.num_programs(0) - 1)
    def _():
        out_ref[:, out_ref.shape[1] - LANES :] = gate_ref[...]


def input_rows(h, wg, wu, gate):
    _, slots, ff = h.shape
    wide = wg.shape[0] + LANES
    blk = wide // 3
    weights = pl.BlockSpec((blk, ff), lambda j: (j, 0))
    return pl.pallas_call(
        input_kernel,
        grid=(3,),
        in_specs=[
            pl.BlockSpec((2, slots, ff), lambda j: (0, 0, 0)),
            weights,
            weights,
            pl.BlockSpec((slots, LANES), lambda j: (0, 0)),
        ],
        out_specs=pl.BlockSpec((slots, blk), lambda j: (0, j)),
        out_shape=jax.ShapeDtypeStruct((slots, wide), BF),
        compiler_params=params(),
        name="input_rows",
    )(h, wg, wu, gate)


def part_kernel(own_ids, mate_ids, ff_ids, own_ref, mate_ref, rhs_ref, rhs_mate_ref, out_ref, *, lo, hi):
    del own_ids, mate_ids, ff_ids
    out_ref[0] = (
        dot_tn(own_ref[:, lo:hi], rhs_ref[0]) + dot_tn(mate_ref[:, lo:hi], rhs_mate_ref[0])
    ).astype(BF)


def partials(own, mate, width, lo, hi, rhs, rhs_mate, own_ids, mate_ids, ff_ids):
    steps = own_ids.shape[0]
    slots = own.shape[0]
    ff = rhs.shape[2]
    rhs_spec = pl.BlockSpec((1, slots, ff), lambda i, own_ids, mate_ids, ff_ids: (ff_ids[i], 0, 0))
    return pl.pallas_call(
        functools.partial(part_kernel, lo=lo, hi=hi),
        grid_spec=pltpu.PrefetchScalarGridSpec(
            num_scalar_prefetch=3,
            grid=(steps,),
            in_specs=[
                pl.BlockSpec((slots, width), lambda i, own_ids, mate_ids, ff_ids: (0, own_ids[i])),
                pl.BlockSpec((slots, width), lambda i, own_ids, mate_ids, ff_ids: (0, mate_ids[i])),
                rhs_spec,
                rhs_spec,
            ],
            out_specs=pl.BlockSpec((1, hi - lo, ff), lambda i, own_ids, mate_ids, ff_ids: (i, 0, 0)),
        ),
        out_shape=jax.ShapeDtypeStruct((steps, hi - lo, ff), BF),
        compiler_params=params(),
        name="partials",
    )(own_ids, mate_ids, ff_ids, own, mate, rhs, rhs_mate)


def unpack_kernel(hot_ref, ids_ref, rows_ref, gates_ref, out_ref, gate_ref):
    out_ref[...] = dot_tn(hot_ref[...], rows_ref[...]).astype(BF)

    @pl.when(pl.program_id(0) == 0)
    def _():
        hot = hot_ref[...]
        expert = lax.broadcasted_iota(jnp.int32, hot.shape, 0) // CAP
        for k in range(2):
            chosen = jnp.where(expert == ids_ref[k : k + 1, :], hot.astype(F32), 0.0).astype(BF)
            gate_ref[k : k + 1, :] = dot_tn(gates_ref[...], chosen)[0:1, :].astype(BF)


def unpack(hot, ids, back, width):
    slots, tok_dev = hot.shape
    steps = 4
    whole = lambda shape: pl.BlockSpec(shape, lambda i: (0, 0))
    return pl.pallas_call(
        unpack_kernel,
        grid=(steps,),
        in_specs=[
            whole((slots, tok_dev)),
            whole((2, tok_dev)),
            pl.BlockSpec((slots, width // steps), lambda i: (0, i)),
            pl.BlockSpec((slots, LANES), lambda i: (0, width // LANES)),
        ],
        out_specs=[pl.BlockSpec((tok_dev, width // steps), lambda i: (0, i)), whole((2, tok_dev))],
        out_shape=[jax.ShapeDtypeStruct((tok_dev, width), BF), jax.ShapeDtypeStruct((2, tok_dev), BF)],
        compiler_params=params(),
        name="unpack",
    )(hot, ids, back, back)


UP = [(i, (i + 2) % 8) for i in range(8)]
DOWN = [(i, (i - 2) % 8) for i in range(8)]
SWAP = [(i, i ^ 1) for i in range(8)]


def ring(parts, perm):
    total = parts[0]
    for part in parts[1:]:
        arrived = lax.ppermute(total, "dp", perm)
        total = (arrived.astype(F32) + part.astype(F32)).astype(BF)
    return total


def body(tokens_in, out_grad, expert_ids, gate_probs, gate_up, down_proj):
    width = tokens_in.shape[1]
    owners = lax.axis_size("expert")
    ff = gate_up.shape[3]
    slots = owners * CAP
    me = lax.axis_index("dp")
    z, core = me // 2, me % 2

    ids = expert_ids.T
    first, second, hot = pack(ids, gate_probs.T, tokens_in, out_grad, slots)

    def exchange(rows):
        wide = rows.shape[1]
        got = lax.all_to_all(rows.reshape(owners, CAP, wide), "expert", split_axis=0, concat_axis=0, tiled=True)
        return got.reshape(slots, wide)

    first = exchange(first)
    second = exchange(second)

    wg = gate_up[:, 0, 0, :]
    wu = gate_up[:, 1, 0, :]
    wd = down_proj[:, 0, :]
    wd_b = wd.reshape(SLICES, SLICE, ff)[:, PART_A:].reshape(SLICES * PART_B, ff)

    order = ((z + jnp.array([3, 2, 1, 0])) % 4).astype(jnp.int32)
    all_z = jnp.arange(4, dtype=jnp.int32)
    theirs = 2 * all_z + (1 - core)
    none = jnp.zeros((4,), jnp.int32)

    mate_first = lax.ppermute(pick(first, theirs, GROUP), "dp", SWAP)
    u_a, c1, c2, p, gp = pre(first, wg, wu, wd)
    gp = gp[None]
    gp_mate = lax.ppermute(gp, "dp", SWAP)
    down_a = partials(first, mate_first, GROUP, SLICE, GROUP, gp, gp_mate, 2 * order + core, order, none)
    half = PART_A // 2
    grad_a = jnp.concatenate(
        [
            ring([down_a[j, :half] for j in (0, 1, 2, 3)], UP),
            ring([down_a[j, half:] for j in (2, 1, 0, 3)], DOWN),
        ],
        axis=0,
    )

    mate_second = lax.ppermute(pick(second, theirs, PART_B), "dp", SWAP)
    h, gate_rows = hidden(second, wd_b, u_a, c1, c2, p)
    h_mate = lax.ppermute(h, "dp", SWAP)
    down_b = partials(second, mate_second, PART_B, 0, PART_B, gp, gp_mate, 2 * order + core, order, none)

    pick_z = jnp.stack([order[0], order[2]])
    pick_f = jnp.array([0, 1], jnp.int32)
    both_1 = partials(first, mate_first, GROUP, 0, SLICE, h, h_mate, 2 * pick_z + core, pick_z, pick_f)
    back = exchange(input_rows(h, wg, wu, gate_rows))
    rest_z = jnp.stack([order[1], order[1], order[2], order[0], order[3], order[3]])
    rest_f = jnp.array([0, 1, 0, 1, 0, 1], jnp.int32)
    both_2 = partials(first, mate_first, GROUP, 0, SLICE, h, h_mate, 2 * rest_z + core, rest_z, rest_f)

    cut = SLICE // 2
    half = PART_B // 2
    ring_gate = [both_1[0], both_2[0], both_2[2], both_2[4]]
    ring_up = [both_1[1], both_2[1], both_2[3], both_2[5]]
    down_up = [down_b[j, :half] for j in (0, 1, 2, 3)]
    down_dn = [down_b[j, half:] for j in (2, 1, 0, 3)]
    gate_lo = ring([t[:cut] for t in ring_gate], UP)
    up_lo = ring([t[:cut] for t in ring_up], DOWN)
    gate_hi = ring([jnp.concatenate([t[cut:], d], axis=0) for t, d in zip(ring_gate, down_up)], UP)
    up_hi = ring([jnp.concatenate([t[cut:], d], axis=0) for t, d in zip(ring_up, down_dn)], DOWN)

    grad_gate = jnp.concatenate([gate_lo, gate_hi[:cut]], axis=0)
    grad_up = jnp.concatenate([up_lo, up_hi[:cut]], axis=0)
    gate_up_grad = jnp.stack([grad_gate, grad_up], axis=1)[:, :, None, :]
    down_grad = jnp.concatenate([grad_a, gate_hi[cut:], up_hi[cut:]], axis=0)[:, None, :]

    input_grad, gate_grad = unpack(hot, ids, back, width)
    return (input_grad, gate_grad.T, gate_up_grad, down_grad)


def solution(mesh):
    placed = (
        P(("dp", "expert"), None),
        P(("dp", "expert"), None),
        P(("dp", "expert"), None),
        P(("dp", "expert"), None),
        P(None, None, "expert", None),
        P(None, "expert", None),
    )
    return jax.shard_map(
        body,
        mesh=mesh,
        in_specs=placed,
        out_specs=(
            P(("dp", "expert"), None),
            P(("dp", "expert"), None),
            P("dp", None, "expert", None),
            P("dp", "expert", None),
        ),
        check_vma=False,
    )
```

```python
import functools

import jax
import jax.numpy as jnp
from jax import lax
from jax.experimental import pallas as pl
from jax.experimental.pallas import tpu as pltpu
from jax.sharding import PartitionSpec as P

BF = jnp.bfloat16
F32 = jnp.float32
SLICE = 512
PART_A = 256
PART_B = SLICE - PART_A
GROUP = SLICE + PART_A
SLICES = 8
CAP = 32
LANES = 128


def params(mib):
    return pltpu.CompilerParams(vmem_limit_bytes=mib * 1024 * 1024)


def in_hbm(x):
    return pltpu.with_memory_space_constraint(x, pltpu.HBM)


def dot_nn(a, b):
    return lax.dot_general(a, b, (((1,), (0,)), ((), ())), preferred_element_type=F32)


def dot_nt(a, b):
    return lax.dot_general(a, b, (((1,), (1,)), ((), ())), preferred_element_type=F32)


def dot_tn(a, b):
    return lax.dot_general(a, b, (((0,), (0,)), ((), ())), preferred_element_type=F32)


def pack_kernel(ids_ref, gates_ref, tok_ref, dy_ref, first_ref, second_ref, hot_ref, *, step_experts):
    tokens = ids_ref.shape[1]
    base = pl.program_id(0) * step_experts
    expert = lax.broadcasted_iota(jnp.int32, (8, tokens), 0) + base
    zero = jnp.zeros((8, tokens), F32)
    is_0 = ids_ref[0:1, :] == expert
    is_1 = ids_ref[1:2, :] == expert
    named = is_0 | is_1
    member = jnp.where(named, 1.0, 0.0).astype(BF)
    row = lax.broadcasted_iota(jnp.int32, (tokens, tokens), 0)
    col = lax.broadcasted_iota(jnp.int32, (tokens, tokens), 1)
    earlier = jnp.where(row < col, 1.0, 0.0).astype(BF)
    place = jnp.where(named, dot_nn(member, earlier), -1.0)
    gates = gates_ref[...].astype(F32)
    weight = jnp.where(is_0, gates[0:1, :], zero) + jnp.where(is_1, gates[1:2, :], zero)
    rows = step_experts * CAP
    place_all = jnp.broadcast_to(place[:step_experts, None, :], (step_experts, CAP, tokens)).reshape(rows, tokens)
    weight_all = jnp.broadcast_to(weight[:step_experts, None, :], (step_experts, CAP, tokens)).reshape(rows, tokens)
    slot = (lax.broadcasted_iota(jnp.int32, (rows, tokens), 0) % CAP).astype(F32)
    hot = jnp.where(place_all == slot, 1.0, 0.0)
    slot_gate = jnp.sum(hot * weight_all, axis=1, keepdims=True)
    first_ref[:, SLICES * GROUP :] = jnp.broadcast_to(slot_gate, (rows, LANES)).astype(BF)
    hot = hot.astype(BF)
    hot_ref[...] = hot
    for q in range(SLICES):
        cols = slice(q * SLICE, (q + 1) * SLICE)
        first_ref[:, q * GROUP : q * GROUP + SLICE] = dot_nn(hot, tok_ref[:, cols]).astype(BF)
        grads = dot_nn(hot, dy_ref[:, cols]).astype(BF)
        first_ref[:, q * GROUP + SLICE : (q + 1) * GROUP] = grads[:, :PART_A]
        second_ref[:, q * PART_B : (q + 1) * PART_B] = grads[:, PART_A:]


def pack(ids, gates, tokens_in, out_grad, slots):
    steps = 4
    tok_dev, width = tokens_in.shape
    rows = slots // steps
    wide = SLICES * GROUP + LANES
    whole = lambda shape: pl.BlockSpec(shape, lambda i: (0, 0))
    return pl.pallas_call(
        functools.partial(pack_kernel, step_experts=rows // CAP),
        grid=(steps,),
        in_specs=[whole((2, tok_dev)), whole((2, tok_dev)), whole((tok_dev, width)), whole((tok_dev, width))],
        out_specs=[
            pl.BlockSpec((rows, wide), lambda i: (i, 0)),
            pl.BlockSpec((rows, SLICES * PART_B), lambda i: (i, 0)),
            pl.BlockSpec((rows, tok_dev), lambda i: (i, 0)),
        ],
        out_shape=[
            pltpu.HBM((slots, wide), BF),
            pltpu.HBM((slots, SLICES * PART_B), BF),
            pltpu.HBM((slots, tok_dev), BF),
        ],
        compiler_params=params(24),
        name="pack",
    )(in_hbm(ids), in_hbm(gates), in_hbm(tokens_in), in_hbm(out_grad))


def pre_kernel(rows_ref, gate_ref, w_ref, wd_ref, u_ref, c1_ref, c2_ref, p_ref, gp_ref, pg_acc, pu_acc, *, per):
    step = pl.program_id(0)

    @pl.when(step == 0)
    def _():
        pg_acc[...] = jnp.zeros_like(pg_acc)
        pu_acc[...] = jnp.zeros_like(pu_acc)
        u_ref[...] = jnp.zeros_like(u_ref)

    x = jnp.concatenate([rows_ref[:, k * GROUP : k * GROUP + SLICE] for k in range(per)], axis=1)
    pg_acc[...] += dot_nn(x, w_ref[0])
    pu_acc[...] += dot_nn(x, w_ref[1])
    dy = jnp.concatenate([rows_ref[:, k * GROUP + SLICE : (k + 1) * GROUP] for k in range(per)], axis=1)
    u_ref[...] += dot_nn(dy, wd_ref[...].reshape(per * PART_A, wd_ref.shape[3]))

    @pl.when(step == pl.num_programs(0) - 1)
    def _():
        chunk = 32

        def one(i, carry):
            at = pl.ds(pl.multiple_of(i * chunk, chunk), chunk)
            pg = pg_acc[at, :]
            pu = pu_acc[at, :]
            g = gate_ref[at, :].astype(F32)[:, :1]
            s = jax.nn.sigmoid(pg)
            a = pg * s
            product = a * pu
            p_ref[at, :] = product.astype(BF)
            gp_ref[at, :] = (g * product).astype(BF)
            c1_ref[at, :] = g * (pu * s * (1.0 + pg * (1.0 - s)))
            c2_ref[at, :] = g * a
            return carry

        lax.fori_loop(0, pg_acc.shape[0] // chunk, one, 0)


def pre(first, w, wd):
    slots = first.shape[0]
    ff = wd.shape[3]
    per = 2
    whole = pl.BlockSpec((slots, ff), lambda q: (0, 0))
    return pl.pallas_call(
        functools.partial(pre_kernel, per=per),
        grid=(SLICES // per,),
        in_specs=[
            pl.BlockSpec((slots, per * GROUP), lambda q: (0, q)),
            pl.BlockSpec((slots, LANES), lambda q: (0, SLICES * GROUP // LANES)),
            pl.BlockSpec((2, per * SLICE, ff), lambda q: (0, q, 0)),
            pl.BlockSpec((per, 1, PART_A, ff), lambda q: (q, 0, 0, 0)),
        ],
        out_specs=[whole] * 5,
        out_shape=[
            jax.ShapeDtypeStruct((slots, ff), F32),
            jax.ShapeDtypeStruct((slots, ff), F32),
            jax.ShapeDtypeStruct((slots, ff), F32),
            jax.ShapeDtypeStruct((slots, ff), BF),
            jax.ShapeDtypeStruct((slots, ff), BF),
        ],
        scratch_shapes=[pltpu.VMEM((slots, ff), F32)] * 2,
        compiler_params=params(36),
        name="pre",
    )(first, first, w, wd)


def hidden_kernel(dy_ref, wd_ref, u_ref, c1_ref, c2_ref, p_ref, h_ref, gate_ref, u_acc, gate_acc):
    step = pl.program_id(0)
    u_acc[...] = u_ref[...] + dot_nn(dy_ref[...], wd_ref[...].reshape(dy_ref.shape[1], wd_ref.shape[3]))

    @pl.when(step == 0)
    def _():
        gate_acc[...] = jnp.zeros_like(gate_acc)

    chunk = 64

    def one(i, carry):
        at = pl.ds(pl.multiple_of(i * chunk, chunk), chunk)
        u = u_acc[at, :]
        h_ref[0, at, :] = (u * c1_ref[at, :]).astype(BF)
        h_ref[1, at, :] = (u * c2_ref[at, :]).astype(BF)
        both = u * p_ref[at, :].astype(F32)
        folded = both[:, :LANES]
        for k in range(1, both.shape[1] // LANES):
            folded += both[:, k * LANES : (k + 1) * LANES]
        gate_acc[at, :] += folded
        return carry

    lax.fori_loop(0, u_acc.shape[0] // chunk, one, 0)

    @pl.when(step == pl.num_programs(0) - 1)
    def _():
        total = jnp.sum(gate_acc[...], axis=1, keepdims=True)
        gate_ref[...] = jnp.broadcast_to(total, gate_ref.shape).astype(BF)


def hidden(second, wd, u_a, c1, c2, p):
    slots, ff = p.shape
    blk = 256
    col = pl.BlockSpec((slots, blk), lambda j: (0, j))
    depth = second.shape[1]
    return pl.pallas_call(
        hidden_kernel,
        grid=(ff // blk,),
        in_specs=[
            pl.BlockSpec((slots, depth), lambda j: (0, 0)),
            pl.BlockSpec((SLICES, 1, PART_B, blk), lambda j: (0, 1, 0, j)),
            col,
            col,
            col,
            col,
        ],
        out_specs=[pl.BlockSpec((2, slots, blk), lambda j: (0, 0, j)), pl.BlockSpec((slots, LANES), lambda j: (0, 0))],
        out_shape=[jax.ShapeDtypeStruct((2, slots, ff), BF), jax.ShapeDtypeStruct((slots, LANES), BF)],
        scratch_shapes=[pltpu.VMEM((slots, blk), F32), pltpu.VMEM((slots, LANES), F32)],
        compiler_params=params(24),
        name="hidden",
    )(second, wd, u_a, c1, c2, p)


def input_kernel(h_ref, w_ref, gate_ref, out_ref):
    out_ref[...] = (dot_nt(h_ref[0], w_ref[0]) + dot_nt(h_ref[1], w_ref[1])).astype(BF)

    @pl.when(pl.program_id(0) == pl.num_programs(0) - 1)
    def _():
        out_ref[:, out_ref.shape[1] - LANES :] = gate_ref[...]


def input_rows(h, w, gate):
    _, slots, ff = h.shape
    wide = w.shape[1] + LANES
    steps = 11
    blk = wide // steps
    return pl.pallas_call(
        input_kernel,
        grid=(steps,),
        in_specs=[
            pl.BlockSpec((2, slots, ff), lambda j: (0, 0, 0)),
            pl.BlockSpec((2, blk, ff), lambda j: (0, j, 0)),
            pl.BlockSpec((slots, LANES), lambda j: (0, 0)),
        ],
        out_specs=pl.BlockSpec((slots, blk), lambda j: (0, j)),
        out_shape=pltpu.HBM((slots, wide), BF),
        compiler_params=params(24),
        name="input_rows",
    )(h, w, gate)


def down_kernel(me_ref, own_ref, mate_ref, gp_ref, gp_mate_ref, up_ref, dn_ref):
    del me_ref
    part = (dot_tn(own_ref[...], gp_ref[...]) + dot_tn(mate_ref[...], gp_mate_ref[...])).astype(BF)
    up_ref[0] = part[: PART_A // 2]
    dn_ref[0] = part[PART_A // 2 :]


def down_slice(me_ref, step):
    me = me_ref[0]
    return 2 * ((me // 2 + 3 - step) % 4) + me % 2


def down_parts(me, own, mate, gp, gp_mate):
    slots, ff = gp.shape
    rows = pl.BlockSpec((slots, PART_A), lambda i, me: (0, 3 * down_slice(me, i) + 2))
    whole = pl.BlockSpec((slots, ff), lambda i, me: (0, 0))
    out = pl.BlockSpec((1, PART_A // 2, ff), lambda i, me: (i, 0, 0))
    return pl.pallas_call(
        down_kernel,
        grid_spec=pltpu.PrefetchScalarGridSpec(
            num_scalar_prefetch=1, grid=(4,), in_specs=[rows, rows, whole, whole], out_specs=[out, out]
        ),
        out_shape=[jax.ShapeDtypeStruct((4, PART_A // 2, ff), BF)] * 2,
        compiler_params=params(16),
        name="down_parts",
    )(me, own, mate, gp, gp_mate)


UNIT = SLICE // 2
EXTRA = PART_B // 4


def unit_part(own_ref, mate_ref, dy_ref, dy_mate_ref, h_ref, h_mate_ref, gp_ref, gp_mate_ref, out_ref):
    ff = gp_ref.shape[1]
    for k in range(2):
        part = dot_tn(own_ref[...], h_ref[k]) + dot_tn(mate_ref[...], h_mate_ref[k])
        out_ref[:UNIT, k * ff : (k + 1) * ff] = part.astype(BF)
    down = (dot_tn(dy_ref[...], gp_ref[...]) + dot_tn(dy_mate_ref[...], gp_mate_ref[...])).astype(BF)
    out_ref[UNIT:, :ff] = down[:EXTRA]
    out_ref[UNIT:, ff:] = down[EXTRA:]


def head_kernel(me_ref, *refs):
    del me_ref
    ins, (up_ref, dn_ref) = refs[:8], refs[8:]

    @pl.when(pl.program_id(0) == 0)
    def _():
        unit_part(*ins, up_ref)

    @pl.when(pl.program_id(0) == 1)
    def _():
        unit_part(*ins, dn_ref)


def rest_kernel(me_ref, *refs):
    del me_ref
    unit_part(*refs[:8], refs[8].at[0])


def units(me, first, mate_first, second, mate_second, h, h_mate, gp, gp_mate, head):
    _, slots, ff = h.shape

    def at(i, me_ref):
        me = me_ref[0]
        hop = (0 if head else 1) + i // 2
        z = me // 2
        turn = jnp.where(i % 2 == 0, z + 3 - hop, z + 1 + hop) % 4
        return 2 * turn + me % 2

    rows = pl.BlockSpec((slots, UNIT), lambda i, me: (0, 3 * at(i, me) + i % 2))
    grads = pl.BlockSpec((slots, PART_B // 2), lambda i, me: (0, 2 * at(i, me) + i % 2))
    hid = pl.BlockSpec((2, slots, ff), lambda i, me: (0, 0, 0))
    whole = pl.BlockSpec((slots, ff), lambda i, me: (0, 0))
    shape = (UNIT + EXTRA, 2 * ff)
    if head:
        steps = 2
        out_specs = [pl.BlockSpec(shape, lambda i, me: (0, 0))] * 2
        out_shape = [jax.ShapeDtypeStruct(shape, BF)] * 2
    else:
        steps = 6
        out_specs = pl.BlockSpec((1,) + shape, lambda i, me: (i, 0, 0))
        out_shape = jax.ShapeDtypeStruct((6,) + shape, BF)
    return pl.pallas_call(
        head_kernel if head else rest_kernel,
        grid_spec=pltpu.PrefetchScalarGridSpec(
            num_scalar_prefetch=1,
            grid=(steps,),
            in_specs=[rows, rows, grads, grads, hid, hid, whole, whole],
            out_specs=out_specs,
        ),
        out_shape=out_shape,
        compiler_params=params(24),
        name="units_head" if head else "units_rest",
    )(me, first, mate_first, second, mate_second, h, h_mate, gp, gp_mate)


def unpack_kernel(hot_ref, ids_ref, rows_ref, gates_ref, out_ref, gate_ref):
    out_ref[...] = dot_tn(hot_ref[...], rows_ref[...]).astype(BF)

    @pl.when(pl.program_id(0) == 0)
    def _():
        hot = hot_ref[...]
        expert = lax.broadcasted_iota(jnp.int32, hot.shape, 0) // CAP
        for k in range(2):
            chosen = jnp.where(expert == ids_ref[k : k + 1, :], hot.astype(F32), 0.0).astype(BF)
            gate_ref[k : k + 1, :] = dot_tn(gates_ref[...], chosen)[0:1, :].astype(BF)


def unpack(hot, ids, back, width):
    slots, tok_dev = hot.shape
    steps = 4
    whole = lambda shape: pl.BlockSpec(shape, lambda i: (0, 0))
    return pl.pallas_call(
        unpack_kernel,
        grid=(steps,),
        in_specs=[
            whole((slots, tok_dev)),
            whole((2, tok_dev)),
            pl.BlockSpec((slots, width // steps), lambda i: (0, i)),
            pl.BlockSpec((slots, LANES), lambda i: (0, width // LANES)),
        ],
        out_specs=[pl.BlockSpec((tok_dev, width // steps), lambda i: (0, i)), whole((2, tok_dev))],
        out_shape=[jax.ShapeDtypeStruct((tok_dev, width), BF), jax.ShapeDtypeStruct((2, tok_dev), BF)],
        compiler_params=params(16),
        name="unpack",
    )(hot, ids, in_hbm(back), in_hbm(back))


UP = [(i, (i + 2) % 8) for i in range(8)]
DOWN = [(i, (i - 2) % 8) for i in range(8)]
SWAP = [(i, i ^ 1) for i in range(8)]


def ring(parts, perm):
    total = parts[0]
    for part in parts[1:]:
        arrived = lax.ppermute(total, "dp", perm)
        total = (arrived.astype(F32) + part.astype(F32)).astype(BF)
    return total


def body(tokens_in, out_grad, expert_ids, gate_probs, gate_up, down_proj):
    width = tokens_in.shape[1]
    owners = lax.axis_size("expert")
    ff = gate_up.shape[3]
    slots = owners * CAP
    me = lax.axis_index("dp")

    ids = expert_ids.T
    first, second, hot = pack(ids, gate_probs.T, tokens_in, out_grad, slots)

    def exchange(rows):
        wide = rows.shape[1]
        got = lax.all_to_all(rows.reshape(owners, CAP, wide), "expert", split_axis=0, concat_axis=0, tiled=True)
        return got.reshape(slots, wide)

    def swap(x):
        return lax.ppermute(x, "dp", SWAP)

    first, gate_up, down_proj, me = lax.optimization_barrier((exchange(first), gate_up, down_proj, me))
    second = exchange(second)
    me = me.reshape(1).astype(jnp.int32)
    mate_first = swap(first)
    w = jnp.transpose(gate_up[:, :, 0], (1, 0, 2))
    wd = down_proj.reshape(SLICES, 2, PART_A, ff)
    u_a, c1, c2, p, gp = pre(first, w, wd)
    gp_mate = swap(gp)
    down_up, down_dn = down_parts(me, first, mate_first, gp, gp_mate)
    second, down_up, down_dn = lax.optimization_barrier((second, down_up, down_dn))
    grad_a = jnp.concatenate(
        [ring([down_up[j] for j in (0, 1, 2, 3)], UP), ring([down_dn[j] for j in (2, 1, 0, 3)], DOWN)], axis=0
    )

    mate_second = swap(second)
    h, gate_rows = hidden(second, wd, u_a, c1, c2, p)
    h_mate = swap(h)
    head_up, head_dn = units(me, first, mate_first, second, mate_second, h, h_mate, gp, gp_mate, True)
    h, head_up, head_dn = lax.optimization_barrier((h, head_up, head_dn))
    back = exchange(input_rows(h, w, gate_rows))
    rest = units(me, first, mate_first, second, mate_second, h, h_mate, gp, gp_mate, False)
    sum_up = ring([head_up, rest[0], rest[2], rest[4]], UP)
    sum_dn = ring([head_dn, rest[1], rest[3], rest[5]], DOWN)

    sums = jnp.concatenate([sum_up[:UNIT], sum_dn[:UNIT]], axis=0)
    gate_up_grad = sums.reshape(SLICE, 2, 1, ff)
    down_b = [t[UNIT:, k * ff : (k + 1) * ff] for t in (sum_up, sum_dn) for k in range(2)]
    down_grad = jnp.concatenate([grad_a] + down_b, axis=0)[:, None, :]

    input_grad, gate_grad = unpack(hot, ids, back, width)
    return (input_grad, gate_grad.T, gate_up_grad, down_grad)


def solution(mesh):
    placed = (
        P(("dp", "expert"), None),
        P(("dp", "expert"), None),
        P(("dp", "expert"), None),
        P(("dp", "expert"), None),
        P(None, None, "expert", None),
        P(None, "expert", None),
    )
    return jax.shard_map(
        body,
        mesh=mesh,
        in_specs=placed,
        out_specs=(
            P(("dp", "expert"), None),
            P(("dp", "expert"), None),
            P("dp", None, "expert", None),
            P("dp", "expert", None),
        ),
        check_vma=False,
    )
```

```python
import functools

import jax
import jax.numpy as jnp
from jax import lax
from jax.experimental import pallas as pl
from jax.experimental.pallas import tpu as pltpu
from jax.sharding import PartitionSpec as P

BF = jnp.bfloat16
F32 = jnp.float32
SLICE = 512
PART_A = 256
PART_B = SLICE - PART_A
GROUP = SLICE + PART_A
SLICES = 8
CAP = 32
LANES = 128
PACK_STEPS = 4
PRE_PER = 2
INPUT_BLOCK = 512
HIDDEN_BLOCK = 256


def params(mib):
    return pltpu.CompilerParams(vmem_limit_bytes=mib * 1024 * 1024)


def in_hbm(x):
    return pltpu.with_memory_space_constraint(x, pltpu.HBM)


def dot_nn(a, b):
    return lax.dot_general(a, b, (((1,), (0,)), ((), ())), preferred_element_type=F32)


def dot_nt(a, b):
    return lax.dot_general(a, b, (((1,), (1,)), ((), ())), preferred_element_type=F32)


def dot_tn(a, b):
    return lax.dot_general(a, b, (((0,), (0,)), ((), ())), preferred_element_type=F32)


def pack_kernel(ids_ref, gates_ref, tok_ref, dy_ref, first_ref, second_ref, hot_ref, *, step_experts):
    tokens = ids_ref.shape[1]
    base = pl.program_id(0) * step_experts
    expert = lax.broadcasted_iota(jnp.int32, (8, tokens), 0) + base
    zero = jnp.zeros((8, tokens), F32)
    is_0 = ids_ref[0:1, :] == expert
    is_1 = ids_ref[1:2, :] == expert
    named = is_0 | is_1
    member = jnp.where(named, 1.0, 0.0).astype(BF)
    row = lax.broadcasted_iota(jnp.int32, (tokens, tokens), 0)
    col = lax.broadcasted_iota(jnp.int32, (tokens, tokens), 1)
    earlier = jnp.where(row < col, 1.0, 0.0).astype(BF)
    place = jnp.where(named, dot_nn(member, earlier), -1.0)
    gates = gates_ref[...].astype(F32)
    weight = jnp.where(is_0, gates[0:1, :], zero) + jnp.where(is_1, gates[1:2, :], zero)
    rows = step_experts * CAP
    place_all = jnp.broadcast_to(place[:step_experts, None, :], (step_experts, CAP, tokens)).reshape(rows, tokens)
    weight_all = jnp.broadcast_to(weight[:step_experts, None, :], (step_experts, CAP, tokens)).reshape(rows, tokens)
    slot = (lax.broadcasted_iota(jnp.int32, (rows, tokens), 0) % CAP).astype(F32)
    hot = jnp.where(place_all == slot, 1.0, 0.0)
    slot_gate = jnp.sum(hot * weight_all, axis=1, keepdims=True)
    first_ref[:, SLICES * GROUP :] = jnp.broadcast_to(slot_gate, (rows, LANES)).astype(BF)
    hot = hot.astype(BF)
    hot_ref[...] = hot
    for q in range(SLICES):
        cols = slice(q * SLICE, (q + 1) * SLICE)
        first_ref[:, q * GROUP : q * GROUP + SLICE] = dot_nn(hot, tok_ref[:, cols]).astype(BF)
        grads = dot_nn(hot, dy_ref[:, cols]).astype(BF)
        first_ref[:, q * GROUP + SLICE : (q + 1) * GROUP] = grads[:, :PART_A]
        second_ref[:, q * PART_B : (q + 1) * PART_B] = grads[:, PART_A:]


def pack(ids, gates, tokens_in, out_grad, slots):
    steps = PACK_STEPS
    tok_dev, width = tokens_in.shape
    rows = slots // steps
    wide = SLICES * GROUP + LANES
    whole = lambda shape: pl.BlockSpec(shape, lambda i: (0, 0))
    return pl.pallas_call(
        functools.partial(pack_kernel, step_experts=rows // CAP),
        grid=(steps,),
        in_specs=[whole((2, tok_dev)), whole((2, tok_dev)), whole((tok_dev, width)), whole((tok_dev, width))],
        out_specs=[
            pl.BlockSpec((rows, wide), lambda i: (i, 0)),
            pl.BlockSpec((rows, SLICES * PART_B), lambda i: (i, 0)),
            pl.BlockSpec((rows, tok_dev), lambda i: (i, 0)),
        ],
        out_shape=[
            pltpu.HBM((slots, wide), BF),
            pltpu.HBM((slots, SLICES * PART_B), BF),
            pltpu.HBM((slots, tok_dev), BF),
        ],
        compiler_params=params(24),
        name="pack",
    )(in_hbm(ids), in_hbm(gates), in_hbm(tokens_in), in_hbm(out_grad))


def pre_kernel(rows_ref, gate_ref, w_ref, wd_ref, u_ref, c1_ref, c2_ref, p_ref, gp_ref, pg_acc, pu_acc, *, per):
    step = pl.program_id(0)

    @pl.when(step == 0)
    def _():
        pg_acc[...] = jnp.zeros_like(pg_acc)
        pu_acc[...] = jnp.zeros_like(pu_acc)
        u_ref[...] = jnp.zeros_like(u_ref)

    x = jnp.concatenate([rows_ref[:, k * GROUP : k * GROUP + SLICE] for k in range(per)], axis=1)
    pg_acc[...] += dot_nn(x, w_ref[0])
    pu_acc[...] += dot_nn(x, w_ref[1])
    dy = jnp.concatenate([rows_ref[:, k * GROUP + SLICE : (k + 1) * GROUP] for k in range(per)], axis=1)
    u_ref[...] += dot_nn(dy, wd_ref[...].reshape(per * PART_A, wd_ref.shape[3]))

    @pl.when(step == pl.num_programs(0) - 1)
    def _():
        chunk = 32

        def one(i, carry):
            at = pl.ds(pl.multiple_of(i * chunk, chunk), chunk)
            pg = pg_acc[at, :]
            pu = pu_acc[at, :]
            g = gate_ref[at, :].astype(F32)[:, :1]
            s = jax.nn.sigmoid(pg)
            a = pg * s
            product = a * pu
            p_ref[at, :] = product.astype(BF)
            gp_ref[at, :] = (g * product).astype(BF)
            c1_ref[at, :] = g * (pu * s * (1.0 + pg * (1.0 - s)))
            c2_ref[at, :] = g * a
            return carry

        lax.fori_loop(0, pg_acc.shape[0] // chunk, one, 0)


def pre(first, w, wd):
    slots = first.shape[0]
    ff = wd.shape[3]
    per = PRE_PER
    whole = pl.BlockSpec((slots, ff), lambda q: (0, 0))
    return pl.pallas_call(
        functools.partial(pre_kernel, per=per),
        grid=(SLICES // per,),
        in_specs=[
            pl.BlockSpec((slots, per * GROUP), lambda q: (0, q)),
            pl.BlockSpec((slots, LANES), lambda q: (0, SLICES * GROUP // LANES)),
            pl.BlockSpec((2, per * SLICE, ff), lambda q: (0, q, 0)),
            pl.BlockSpec((per, 1, PART_A, ff), lambda q: (q, 0, 0, 0)),
        ],
        out_specs=[whole] * 5,
        out_shape=[
            pltpu.HBM((slots, ff), F32),
            pltpu.HBM((slots, ff), F32),
            pltpu.HBM((slots, ff), F32),
            pltpu.HBM((slots, ff), BF),
            pltpu.HBM((slots, ff), BF),
        ],
        scratch_shapes=[pltpu.VMEM((slots, ff), F32)] * 2,
        compiler_params=params(36),
        name="pre",
    )(*map(in_hbm, (first, first, w, wd)))


def hidden_kernel(dy_ref, wd_ref, u_ref, c1_ref, c2_ref, p_ref, h_ref, gate_ref, u_acc, gate_acc):
    step = pl.program_id(0)
    u_acc[...] = u_ref[...] + dot_nn(dy_ref[...], wd_ref[...].reshape(dy_ref.shape[1], wd_ref.shape[3]))

    @pl.when(step == 0)
    def _():
        gate_acc[...] = jnp.zeros_like(gate_acc)

    chunk = 64

    def one(i, carry):
        at = pl.ds(pl.multiple_of(i * chunk, chunk), chunk)
        u = u_acc[at, :]
        h_ref[0, at, :] = (u * c1_ref[at, :]).astype(BF)
        h_ref[1, at, :] = (u * c2_ref[at, :]).astype(BF)
        both = u * p_ref[at, :].astype(F32)
        folded = both[:, :LANES]
        for k in range(1, both.shape[1] // LANES):
            folded += both[:, k * LANES : (k + 1) * LANES]
        gate_acc[at, :] += folded
        return carry

    lax.fori_loop(0, u_acc.shape[0] // chunk, one, 0)

    @pl.when(step == pl.num_programs(0) - 1)
    def _():
        total = jnp.sum(gate_acc[...], axis=1, keepdims=True)
        gate_ref[...] = jnp.broadcast_to(total, gate_ref.shape).astype(BF)


def hidden(second, wd, u_a, c1, c2, p, gate_at):
    slots, ff = p.shape
    blk = HIDDEN_BLOCK
    col = pl.BlockSpec((slots, blk), lambda j: (0, j))
    depth = second.shape[1]
    return pl.pallas_call(
        hidden_kernel,
        grid=(ff // blk,),
        in_specs=[
            pl.BlockSpec((slots, depth), lambda j: (0, 0)),
            pl.BlockSpec((SLICES, 1, PART_B, blk), lambda j: (0, 1, 0, j)),
            col,
            col,
            col,
            col,
        ],
        out_specs=[pl.BlockSpec((2, slots, blk), lambda j: (0, 0, j)), pl.BlockSpec((slots, LANES), lambda j: (0, gate_at // LANES))],
        out_shape=[pltpu.HBM((2, slots, ff), BF), pltpu.HBM((slots, gate_at + LANES), BF)],
        scratch_shapes=[pltpu.VMEM((slots, blk), F32), pltpu.VMEM((slots, LANES), F32)],
        compiler_params=params(24),
        name="hidden",
    )(*map(in_hbm, (second, wd, u_a, c1, c2, p)))


def input_kernel(h_ref, w_ref, *refs):
    out_ref = refs[-1]
    out_ref[...] = (dot_nt(h_ref[0], w_ref[0]) + dot_nt(h_ref[1], w_ref[1])).astype(BF)


def input_rows(h, w, begin, cols, into=None):
    _, slots, ff = h.shape
    blk = INPUT_BLOCK
    first = begin // blk
    in_specs = [
        pl.BlockSpec((2, slots, ff), lambda j: (0, 0, 0)),
        pl.BlockSpec((2, blk, ff), lambda j: (0, first + j, 0)),
    ]
    args = [in_hbm(h), in_hbm(w)]
    shape = (slots, cols)
    alias = {}
    if into is not None:
        in_specs.append(pl.BlockSpec(memory_space=pltpu.HBM))
        args.append(in_hbm(into))
        shape = into.shape
        alias = {2: 0}
    return pl.pallas_call(
        input_kernel,
        grid=(cols // blk,),
        in_specs=in_specs,
        out_specs=pl.BlockSpec((slots, blk), lambda j: (0, j)),
        out_shape=pltpu.HBM(shape, BF),
        input_output_aliases=alias,
        compiler_params=params(24),
        name="input_rows",
    )(*args)


def down_kernel(me_ref, own_ref, mate_ref, gp_ref, gp_mate_ref, up_ref, dn_ref):
    del me_ref
    part = (dot_tn(own_ref[...], gp_ref[...]) + dot_tn(mate_ref[...], gp_mate_ref[...])).astype(BF)
    up_ref[0] = part[: PART_A // 2]
    dn_ref[0] = part[PART_A // 2 :]


def down_slice(me_ref, step):
    me = me_ref[0]
    return 2 * ((me // 2 + 3 - step) % 4) + me % 2


def down_parts(me, own, mate, gp, gp_mate):
    slots, ff = gp.shape
    rows = pl.BlockSpec((slots, PART_A), lambda i, me: (0, 3 * down_slice(me, i) + 2))
    whole = pl.BlockSpec((slots, ff), lambda i, me: (0, 0))
    out = pl.BlockSpec((1, PART_A // 2, ff), lambda i, me: (i, 0, 0))
    return pl.pallas_call(
        down_kernel,
        grid_spec=pltpu.PrefetchScalarGridSpec(
            num_scalar_prefetch=1, grid=(4,), in_specs=[rows, rows, whole, whole], out_specs=[out, out]
        ),
        out_shape=[pltpu.HBM((4, PART_A // 2, ff), BF)] * 2,
        compiler_params=params(16),
        name="down_parts",
    )(me, *map(in_hbm, (own, mate, gp, gp_mate)))


UNIT = SLICE // 2
EXTRA = PART_B // 4


def unit_part(own_ref, mate_ref, dy_ref, dy_mate_ref, h_ref, h_mate_ref, gp_ref, gp_mate_ref, out_ref):
    ff = gp_ref.shape[1]
    for k in range(2):
        part = dot_tn(own_ref[...], h_ref[k]) + dot_tn(mate_ref[...], h_mate_ref[k])
        out_ref[:UNIT, k * ff : (k + 1) * ff] = part.astype(BF)
    down = (dot_tn(dy_ref[...], gp_ref[...]) + dot_tn(dy_mate_ref[...], gp_mate_ref[...])).astype(BF)
    out_ref[UNIT:, :ff] = down[:EXTRA]
    out_ref[UNIT:, ff:] = down[EXTRA:]


def head_kernel(me_ref, *refs):
    del me_ref
    ins, (up_ref, dn_ref) = refs[:8], refs[8:]

    @pl.when(pl.program_id(0) == 0)
    def _():
        unit_part(*ins, up_ref)

    @pl.when(pl.program_id(0) == 1)
    def _():
        unit_part(*ins, dn_ref)


def rest_kernel(me_ref, *refs):
    del me_ref
    unit_part(*refs[:8], refs[8].at[0])


def units(me, first, mate_first, second, mate_second, h, h_mate, gp, gp_mate, head):
    _, slots, ff = h.shape

    def at(i, me_ref):
        me = me_ref[0]
        hop = (0 if head else 1) + i // 2
        z = me // 2
        turn = jnp.where(i % 2 == 0, z + 3 - hop, z + 1 + hop) % 4
        return 2 * turn + me % 2

    rows = pl.BlockSpec((slots, UNIT), lambda i, me: (0, 3 * at(i, me) + i % 2))
    grads = pl.BlockSpec((slots, PART_B // 2), lambda i, me: (0, 2 * at(i, me) + i % 2))
    hid = pl.BlockSpec((2, slots, ff), lambda i, me: (0, 0, 0))
    whole = pl.BlockSpec((slots, ff), lambda i, me: (0, 0))
    shape = (UNIT + EXTRA, 2 * ff)
    if head:
        steps = 2
        out_specs = [pl.BlockSpec(shape, lambda i, me: (0, 0))] * 2
        out_shape = [pltpu.HBM(shape, BF)] * 2
    else:
        steps = 6
        out_specs = pl.BlockSpec((1,) + shape, lambda i, me: (i, 0, 0))
        out_shape = pltpu.HBM((6,) + shape, BF)
    return pl.pallas_call(
        head_kernel if head else rest_kernel,
        grid_spec=pltpu.PrefetchScalarGridSpec(
            num_scalar_prefetch=1,
            grid=(steps,),
            in_specs=[rows, rows, grads, grads, hid, hid, whole, whole],
            out_specs=out_specs,
        ),
        out_shape=out_shape,
        compiler_params=params(24),
        name="units_head" if head else "units_rest",
    )(me, *map(in_hbm, (first, mate_first, second, mate_second, h, h_mate, gp, gp_mate)))


def unpack_kernel(hot_ref, rows_ref, out_ref):
    out_ref[...] = dot_tn(hot_ref[...], rows_ref[...]).astype(BF)


def unpack_gate_kernel(hot_ref, rows_ref, ids_ref, gates_ref, out_ref, gate_ref):
    unpack_kernel(hot_ref, rows_ref, out_ref)

    @pl.when(pl.program_id(0) == 0)
    def _():
        hot = hot_ref[...]
        expert = lax.broadcasted_iota(jnp.int32, hot.shape, 0) // CAP
        for k in range(2):
            chosen = jnp.where(expert == ids_ref[k : k + 1, :], hot.astype(F32), 0.0).astype(BF)
            gate_ref[k : k + 1, :] = dot_tn(gates_ref[...], chosen)[0:1, :].astype(BF)


def unpack(hot, ids, back, width):
    slots, tok_dev = hot.shape
    blk = 512
    half = width // 2
    whole = lambda shape: pl.BlockSpec(shape, lambda i: (0, 0))
    return pl.pallas_call(
        unpack_gate_kernel,
        grid=(half // blk,),
        in_specs=[
            whole((slots, tok_dev)),
            pl.BlockSpec((slots, blk), lambda i: (0, i)),
            whole((2, tok_dev)),
            pl.BlockSpec((slots, LANES), lambda i: (0, half // LANES)),
        ],
        out_specs=[pl.BlockSpec((tok_dev, blk), lambda i: (0, i)), whole((2, tok_dev))],
        out_shape=[pltpu.HBM((tok_dev, width), BF), pltpu.HBM((2, tok_dev), BF)],
        compiler_params=params(16),
        name="unpack",
    )(*map(in_hbm, (hot, back, ids, back)))


def unpack_tail_kernel(hot_ref, rows_ref, whole_ref, out_ref):
    del whole_ref
    unpack_kernel(hot_ref, rows_ref, out_ref)


def unpack_tail(hot, back, into):
    slots, tok_dev = hot.shape
    blk = 512
    steps = back.shape[1] // blk
    return pl.pallas_call(
        unpack_tail_kernel,
        grid=(steps,),
        in_specs=[
            pl.BlockSpec((slots, tok_dev), lambda i: (0, 0)),
            pl.BlockSpec((slots, blk), lambda i: (0, i)),
            pl.BlockSpec(memory_space=pltpu.HBM),
        ],
        out_specs=pl.BlockSpec((tok_dev, blk), lambda i: (0, steps + i)),
        out_shape=pltpu.HBM(into.shape, BF),
        input_output_aliases={2: 0},
        compiler_params=params(16),
        name="unpack_tail",
    )(*map(in_hbm, (hot, back, into)))


UP = [(i, (i + 2) % 8) for i in range(8)]
DOWN = [(i, (i - 2) % 8) for i in range(8)]
SWAP = [(i, i ^ 1) for i in range(8)]


def ring(parts, perm):
    total = parts[0]
    for part in parts[1:]:
        arrived = lax.ppermute(total, "dp", perm)
        total = (arrived.astype(F32) + part.astype(F32)).astype(BF)
    return total


def body(tokens_in, out_grad, expert_ids, gate_probs, gate_up, down_proj):
    width = tokens_in.shape[1]
    owners = lax.axis_size("expert")
    ff = gate_up.shape[3]
    slots = owners * CAP
    me = lax.axis_index("dp")

    ids = expert_ids.T
    first, second, hot = pack(ids, gate_probs.T, tokens_in, out_grad, slots)

    def exchange(rows):
        wide = rows.shape[1]
        got = lax.all_to_all(rows.reshape(owners, CAP, wide), "expert", split_axis=0, concat_axis=0, tiled=True)
        return got.reshape(slots, wide)

    def swap(x):
        return lax.ppermute(x, "dp", SWAP)

    me = me.reshape(1).astype(jnp.int32)
    first, me = lax.optimization_barrier((first, me))
    first, gate_up, down_proj = lax.optimization_barrier((exchange(first), gate_up, down_proj))
    second = exchange(second)
    mate_first = swap(first)
    w = jnp.transpose(gate_up[:, :, 0], (1, 0, 2))
    wd = down_proj.reshape(SLICES, 2, PART_A, ff)
    u_a, c1, c2, p, gp = pre(first, w, wd)
    gp_mate = swap(gp)
    down_up, down_dn = down_parts(me, first, mate_first, gp, gp_mate)
    arrived_up = lax.ppermute(down_up[0], "dp", UP)
    arrived_dn = lax.ppermute(down_dn[2], "dp", DOWN)
    second, _, _ = lax.optimization_barrier((second, down_up, down_dn))

    half = width // 2
    mate_second = swap(second)
    h, rows_1 = hidden(second, wd, u_a, c1, c2, p, half)
    h_mate = swap(h)
    rows_1 = input_rows(h, w, 0, half, rows_1)
    h_mate, rows_1 = lax.optimization_barrier((h_mate, rows_1))
    back_1 = exchange(rows_1)
    head_up, head_dn = units(me, first, mate_first, second, mate_second, h, h_mate, gp, gp_mate, True)
    h, head_up, head_dn, arrived_up, arrived_dn = lax.optimization_barrier((h, head_up, head_dn, arrived_up, arrived_dn))
    rows_2 = input_rows(h, w, half, half)
    h, rows_2 = lax.optimization_barrier((h, rows_2))
    rest = units(me, first, mate_first, second, mate_second, h, h_mate, gp, gp_mate, False)
    back_2 = exchange(rows_2)
    total = lambda a, b: (a.astype(F32) + b.astype(F32)).astype(BF)
    grad_a = jnp.concatenate(
        [
            ring([total(arrived_up, down_up[1]), down_up[2], down_up[3]], UP),
            ring([total(arrived_dn, down_dn[1]), down_dn[0], down_dn[3]], DOWN),
        ],
        axis=0,
    )
    sum_up = ring([head_up, rest[0], rest[2], rest[4]], UP)
    sum_dn = ring([head_dn, rest[1], rest[3], rest[5]], DOWN)

    sums = jnp.concatenate([sum_up[:UNIT], sum_dn[:UNIT]], axis=0)
    gate_up_grad = sums.reshape(SLICE, 2, 1, ff)
    down_b = [t[UNIT:, k * ff : (k + 1) * ff] for t in (sum_up, sum_dn) for k in range(2)]
    down_grad = jnp.concatenate([grad_a] + down_b, axis=0)[:, None, :]

    input_grad, gate_grad = unpack(hot, ids, back_1, width)
    input_grad = unpack_tail(hot, back_2, input_grad)
    return (input_grad, gate_grad.T, gate_up_grad, down_grad)


def solution(mesh):
    placed = (
        P(("dp", "expert"), None),
        P(("dp", "expert"), None),
        P(("dp", "expert"), None),
        P(("dp", "expert"), None),
        P(None, None, "expert", None),
        P(None, "expert", None),
    )
    return jax.shard_map(
        body,
        mesh=mesh,
        in_specs=placed,
        out_specs=(
            P(("dp", "expert"), None),
            P(("dp", "expert"), None),
            P("dp", None, "expert", None),
            P("dp", "expert", None),
        ),
        check_vma=False,
    )
```

```python
import functools

import jax
import jax.numpy as jnp
from jax import lax
from jax.experimental import pallas as pl
from jax.experimental.pallas import tpu as pltpu
from jax.sharding import PartitionSpec as P

BF = jnp.bfloat16
F32 = jnp.float32
SLICE = 512
PART_A = 256
PART_B = SLICE - PART_A
SLICES = 8
GRADS = SLICES * SLICE
FIRST = GRADS + SLICES * PART_A
CAP = 32
LANES = 128
PACK_STEPS = 2
PRE_PER = 2
INPUT_BLOCK = 1024


def params(mib):
    return pltpu.CompilerParams(vmem_limit_bytes=mib * 1024 * 1024)


def in_hbm(x):
    return pltpu.with_memory_space_constraint(x, pltpu.HBM)


def in_vmem(x):
    return pltpu.with_memory_space_constraint(x, pltpu.VMEM)


def held(shape):
    return pl.BlockSpec(shape, lambda *_: (0,) * len(shape), pipeline_mode=pl.Buffered(1))


def left_in_hbm():
    return pl.BlockSpec(memory_space=pltpu.HBM)


def dot_nn(a, b):
    return lax.dot_general(a, b, (((1,), (0,)), ((), ())), preferred_element_type=F32)


def dot_nt(a, b):
    return lax.dot_general(a, b, (((1,), (1,)), ((), ())), preferred_element_type=F32)


def dot_tn(a, b):
    return lax.dot_general(a, b, (((0,), (0,)), ((), ())), preferred_element_type=F32)


def pack_kernel(ids_ref, gates_ref, tok_ref, dy_ref, first_ref, second_ref, hot_ref, *, step_experts):
    tokens = ids_ref.shape[1]
    base = pl.program_id(0) * step_experts
    expert = lax.broadcasted_iota(jnp.int32, (8, tokens), 0) + base
    zero = jnp.zeros((8, tokens), F32)
    is_0 = ids_ref[0:1, :] == expert
    is_1 = ids_ref[1:2, :] == expert
    named = is_0 | is_1
    member = jnp.where(named, 1.0, 0.0).astype(BF)
    row = lax.broadcasted_iota(jnp.int32, (tokens, tokens), 0)
    col = lax.broadcasted_iota(jnp.int32, (tokens, tokens), 1)
    earlier = jnp.where(row < col, 1.0, 0.0).astype(BF)
    place = jnp.where(named, dot_nn(member, earlier), -1.0)
    gates = gates_ref[...].astype(F32)
    weight = jnp.where(is_0, gates[0:1, :], zero) + jnp.where(is_1, gates[1:2, :], zero)
    rows = step_experts * CAP
    place_all = jnp.broadcast_to(place[:step_experts, None, :], (step_experts, CAP, tokens)).reshape(rows, tokens)
    weight_all = jnp.broadcast_to(weight[:step_experts, None, :], (step_experts, CAP, tokens)).reshape(rows, tokens)
    slot = (lax.broadcasted_iota(jnp.int32, (rows, tokens), 0) % CAP).astype(F32)
    hot = jnp.where(place_all == slot, 1.0, 0.0)
    slot_gate = jnp.sum(hot * weight_all, axis=1, keepdims=True)
    first_ref[:, FIRST:] = jnp.broadcast_to(slot_gate, (rows, LANES)).astype(BF)
    hot = hot.astype(BF)
    hot_ref[...] = hot
    for q in range(SLICES):
        cols = slice(q * SLICE, (q + 1) * SLICE)
        first_ref[:, cols] = dot_nn(hot, tok_ref[:, cols]).astype(BF)
        grads = dot_nn(hot, dy_ref[:, cols]).astype(BF)
        first_ref[:, GRADS + q * PART_A : GRADS + (q + 1) * PART_A] = grads[:, :PART_A]
        second_ref[:, q * PART_B : (q + 1) * PART_B] = grads[:, PART_A:]


def pack(ids, gates, tokens_in, out_grad, slots):
    steps = PACK_STEPS
    tok_dev, width = tokens_in.shape
    rows = slots // steps
    wide = FIRST + LANES
    whole = lambda shape: pl.BlockSpec(shape, lambda i: (0, 0))
    return pl.pallas_call(
        functools.partial(pack_kernel, step_experts=rows // CAP),
        grid=(steps,),
        in_specs=[whole((2, tok_dev)), whole((2, tok_dev)), whole((tok_dev, width)), whole((tok_dev, width))],
        out_specs=[
            pl.BlockSpec((rows, wide), lambda i: (i, 0)),
            pl.BlockSpec((rows, SLICES * PART_B), lambda i: (i, 0)),
            pl.BlockSpec((rows, tok_dev), lambda i: (i, 0)),
        ],
        out_shape=[
            pltpu.HBM((slots, wide), BF),
            pltpu.HBM((slots, SLICES * PART_B), BF),
            pltpu.HBM((slots, tok_dev), BF),
        ],
        compiler_params=params(24),
        name="pack",
    )(in_hbm(ids), in_hbm(gates), in_hbm(tokens_in), in_hbm(out_grad))


def pre_kernel(rows_ref, dy_ref, gate_ref, w_ref, wd_ref, *refs, per):
    outs, (u_acc, pg_acc, pu_acc, p_buf, gp_buf, sems) = refs[:5], refs[5:]
    step = pl.program_id(0)

    @pl.when(step == 0)
    def _():
        pg_acc[...] = jnp.zeros_like(pg_acc)
        pu_acc[...] = jnp.zeros_like(pu_acc)
        u_acc[...] = jnp.zeros_like(u_acc)

    depth = pl.ds(pl.multiple_of(step * per * SLICE, SLICE), per * SLICE)
    u_acc[...] += dot_nn(dy_ref[...], wd_ref[...].reshape(per * PART_A, wd_ref.shape[3]))
    x = rows_ref[...]
    pg_acc[...] += dot_nn(x, w_ref[0, depth, :])
    pu_acc[...] += dot_nn(x, w_ref[1, depth, :])

    @pl.when(step == pl.num_programs(0) - 1)
    def _():
        slots = pg_acc.shape[0]
        chunk, part = 32, slots // 4
        copies = [pltpu.make_async_copy(u_acc, outs[0], sems.at[4, 0])]
        copies[0].start()
        for k in range(4):

            def one(i, carry):
                at = pl.ds(pl.multiple_of(k * part + i * chunk, chunk), chunk)
                pg = pg_acc[at, :]
                pu = pu_acc[at, :]
                g = gate_ref[at, :].astype(F32)[:, :1]
                s = jax.nn.sigmoid(pg)
                a = pg * s
                product = a * pu
                p_buf[at, :] = product.astype(BF)
                gp_buf[at, :] = (g * product).astype(BF)
                pg_acc[at, :] = g * (pu * s * (1.0 + pg * (1.0 - s)))
                pu_acc[at, :] = g * a
                return carry

            lax.fori_loop(0, part // chunk, one, 0)
            for j, (buf, out) in enumerate(zip((pg_acc, pu_acc, p_buf, gp_buf), outs[1:])):
                at = pl.ds(k * part, part)
                copies.append(pltpu.make_async_copy(buf.at[at], out.at[at], sems.at[j, k]))
                copies[-1].start()
        for copy in copies:
            copy.wait()


def pre(first, w, wd):
    slots = first.shape[0]
    ff = wd.shape[3]
    per = PRE_PER
    return pl.pallas_call(
        functools.partial(pre_kernel, per=per),
        grid=(SLICES // per,),
        in_specs=[
            pl.BlockSpec((slots, per * SLICE), lambda q: (0, q)),
            pl.BlockSpec((slots, per * PART_A), lambda q: (0, GRADS // (per * PART_A) + q)),
            pl.BlockSpec((slots, LANES), lambda q: (0, FIRST // LANES)),
            pl.BlockSpec(memory_space=pltpu.VMEM),
            pl.BlockSpec((per, 1, PART_A, ff), lambda q: (q, 0, 0, 0)),
        ],
        out_specs=[left_in_hbm()] * 5,
        out_shape=[pltpu.HBM((slots, ff), t) for t in (F32, F32, F32, BF, BF)],
        scratch_shapes=[pltpu.VMEM((slots, ff), t) for t in (F32, F32, F32, BF, BF)]
        + [pltpu.SemaphoreType.DMA((5, 4))],
        compiler_params=params(24),
        name="pre",
    )(in_hbm(first), in_hbm(first), in_hbm(first), in_vmem(w), in_hbm(wd))


def hidden_kernel(dy_hbm, wd_hbm, u_hbm, c1_hbm, c2_hbm, p_hbm, h_ref, gate_ref, *scratch):
    dy, wd, u_acc, c1, c2, p, gate_acc, sems = scratch
    half = SLICES // 2
    depth = half * PART_B
    wanted = [
        (dy_hbm, dy),
        (wd_hbm.at[:half, 1], wd.at[:half]),
        (wd_hbm.at[half:, 1], wd.at[half:]),
        (u_hbm, u_acc),
        (c1_hbm, c1),
        (c2_hbm, c2),
        (p_hbm, p),
    ]
    copies = [pltpu.make_async_copy(src, dst, sems.at[k]) for k, (src, dst) in enumerate(wanted)]
    for copy in copies:
        copy.start()
    copies[0].wait()
    copies[1].wait()
    copies[3].wait()
    u_acc[...] += dot_nn(dy[:, :depth], wd[:half].reshape(depth, wd.shape[2]))
    copies[2].wait()
    u_acc[...] += dot_nn(dy[:, depth:], wd[half:].reshape(depth, wd.shape[2]))
    for copy in copies[4:]:
        copy.wait()
    chunk = 32

    def one(i, carry):
        at = pl.ds(pl.multiple_of(i * chunk, chunk), chunk)
        u = u_acc[at, :]
        h_ref[0, at, :] = (u * c1[at, :]).astype(BF)
        h_ref[1, at, :] = (u * c2[at, :]).astype(BF)
        both = u * p[at, :].astype(F32)
        folded = both[:, :LANES]
        for k in range(1, both.shape[1] // LANES):
            folded += both[:, k * LANES : (k + 1) * LANES]
        gate_acc[at, :] = folded
        return carry

    lax.fori_loop(0, u_acc.shape[0] // chunk, one, 0)
    total = jnp.sum(gate_acc[...], axis=1, keepdims=True)
    gate_ref[...] = jnp.broadcast_to(total, gate_ref.shape).astype(BF)


def hidden(second, wd, u_a, c1, c2, p, gate_at):
    slots, ff = p.shape
    return pl.pallas_call(
        hidden_kernel,
        grid=(1,),
        in_specs=[pl.BlockSpec(memory_space=pl.ANY)] + [left_in_hbm()] * 5,
        out_specs=[held((2, slots, ff)), pl.BlockSpec((slots, LANES), lambda j: (0, gate_at // LANES))],
        out_shape=[pltpu.HBM((2, slots, ff), BF), pltpu.HBM((slots, gate_at + LANES), BF)],
        scratch_shapes=[
            pltpu.VMEM(second.shape, BF),
            pltpu.VMEM((SLICES, PART_B, ff), BF),
            pltpu.VMEM((slots, ff), F32),
            pltpu.VMEM((slots, ff), F32),
            pltpu.VMEM((slots, ff), F32),
            pltpu.VMEM((slots, ff), BF),
            pltpu.VMEM((slots, LANES), F32),
            pltpu.SemaphoreType.DMA((7,)),
        ],
        compiler_params=params(24),
        name="hidden",
    )(second, *map(in_hbm, (wd, u_a, c1, c2, p)))


def input_kernel(h_ref, w_ref, into_ref, out_ref):
    del into_ref
    out_ref[...] = (dot_nt(h_ref[0], w_ref[0]) + dot_nt(h_ref[1], w_ref[1])).astype(BF)


def input_rows(h, w, begin, cols, into):
    _, slots, ff = h.shape
    blk = INPUT_BLOCK
    first = begin // blk
    return pl.pallas_call(
        input_kernel,
        grid=(cols // blk,),
        in_specs=[held((2, slots, ff)), pl.BlockSpec((2, blk, ff), lambda j: (0, first + j, 0)), left_in_hbm()],
        out_specs=pl.BlockSpec((slots, blk), lambda j: (0, first + j)),
        out_shape=pltpu.HBM(into.shape, BF),
        input_output_aliases={2: 0},
        compiler_params=params(24),
        name="input_rows",
    )(in_hbm(h), in_hbm(w), in_hbm(into))


def down_kernel(rows_ref, gp_ref, out_ref):
    for k in range(2):
        part = dot_tn(rows_ref[:, k * PART_A : (k + 1) * PART_A], gp_ref[...])
        out_ref[k * PART_A : (k + 1) * PART_A] = part.astype(BF)


def down_parts(own, gp):
    slots, ff = gp.shape
    return pl.pallas_call(
        down_kernel,
        grid=(SLICES // 2,),
        in_specs=[pl.BlockSpec((slots, 2 * PART_A), lambda i: (0, GRADS // (2 * PART_A) + i)), held((slots, ff))],
        out_specs=pl.BlockSpec((2 * PART_A, ff), lambda i: (i, 0)),
        out_shape=pltpu.HBM((SLICES * PART_A, ff), BF),
        compiler_params=params(16),
        name="down_parts",
    )(in_hbm(own), in_hbm(gp))


EXTRA = PART_B // 2


def unit_kernel(me_ref, own_ref, mate_ref, dy_ref, dy_mate_ref, h_ref, h_mate_ref, gp_ref, gp_mate_ref, out_ref):
    del me_ref
    ff = gp_ref.shape[1]
    own = own_ref[...]
    mate = mate_ref[...]
    for k in range(2):
        part = dot_tn(own, h_ref[k]) + dot_tn(mate, h_mate_ref[k])
        out_ref[:SLICE, k * ff : (k + 1) * ff] = part.astype(BF)
    down = (dot_tn(dy_ref[...], gp_ref[...]) + dot_tn(dy_mate_ref[...], gp_mate_ref[...])).astype(BF)
    out_ref[SLICE:, :ff] = down[:EXTRA]
    out_ref[SLICE:, ff:] = down[EXTRA:]


def units(me, first, mate_first, second, mate_second, h, h_mate, gp, gp_mate):
    _, slots, ff = h.shape
    rows = pl.BlockSpec((slots, SLICE), lambda i, me: (0, 2 * i + me[0] % 2))
    grads = pl.BlockSpec((slots, PART_B), lambda i, me: (0, 2 * i + me[0] % 2))
    deep = SLICE + EXTRA
    return pl.pallas_call(
        unit_kernel,
        grid_spec=pltpu.PrefetchScalarGridSpec(
            num_scalar_prefetch=1,
            grid=(4,),
            in_specs=[rows, rows, grads, grads] + [held((2, slots, ff))] * 2 + [held((slots, ff))] * 2,
            out_specs=pl.BlockSpec((deep, 2 * ff), lambda i, me: (i, 0)),
        ),
        out_shape=pltpu.HBM((4 * deep, 2 * ff), BF),
        compiler_params=params(20),
        name="units",
    )(me, in_hbm(first), in_hbm(mate_first), second, mate_second, in_hbm(h), h_mate, in_hbm(gp), gp_mate)


def unpack_kernel(hot_ref, rows_ref, ids_ref, gates_ref, out_ref, gate_ref):
    out_ref[...] = dot_tn(hot_ref[...], rows_ref[...]).astype(BF)

    @pl.when(pl.program_id(0) == 0)
    def _():
        hot = hot_ref[...]
        expert = lax.broadcasted_iota(jnp.int32, hot.shape, 0) // CAP
        for k in range(2):
            chosen = jnp.where(expert == ids_ref[k : k + 1, :], hot.astype(F32), 0.0).astype(BF)
            gate_ref[k : k + 1, :] = dot_tn(gates_ref[...], chosen)[0:1, :].astype(BF)


def unpack(hot, ids, back, width):
    slots, tok_dev = hot.shape
    blk = 1024
    whole = lambda shape: pl.BlockSpec(shape, lambda i: (0, 0))
    return pl.pallas_call(
        unpack_kernel,
        grid=(width // blk,),
        in_specs=[
            whole((slots, tok_dev)),
            pl.BlockSpec((slots, blk), lambda i: (0, i)),
            whole((2, tok_dev)),
            pl.BlockSpec((slots, LANES), lambda i: (0, width // LANES)),
        ],
        out_specs=[pl.BlockSpec((tok_dev, blk), lambda i: (0, i)), whole((2, tok_dev))],
        out_shape=[pltpu.HBM((tok_dev, width), BF), pltpu.HBM((2, tok_dev), BF)],
        compiler_params=params(16),
        name="unpack",
    )(*map(in_hbm, (hot, back, ids, back)))


SWAP = [(i, i ^ 1) for i in range(8)]
CHIPS = [[0, 2, 4, 6], [1, 3, 5, 7]]


def body(tokens_in, out_grad, expert_ids, gate_probs, gate_up, down_proj):
    width = tokens_in.shape[1]
    owners = lax.axis_size("expert")
    ff = gate_up.shape[3]
    slots = owners * CAP
    me = lax.axis_index("dp")

    ids = expert_ids.T
    first, second, hot = pack(ids, gate_probs.T, tokens_in, out_grad, slots)

    def exchange(rows):
        wide = rows.shape[1]
        got = lax.all_to_all(rows.reshape(owners, CAP, wide), "expert", split_axis=0, concat_axis=0, tiled=True)
        return got.reshape(slots, wide)

    def swap(x):
        return lax.ppermute(x, "dp", SWAP)

    me = me.reshape(1).astype(jnp.int32)
    first, me = lax.optimization_barrier((first, me))
    first, gate_up, down_proj = lax.optimization_barrier((exchange(first), gate_up, down_proj))
    second = exchange(second)
    mate_first = swap(first)
    w = jnp.transpose(gate_up[:, :, 0], (1, 0, 2))
    wd = down_proj.reshape(SLICES, 2, PART_A, ff)
    u_a, c1, c2, p, gp = pre(first, w, wd)
    gp_mate = swap(gp)

    down_a = down_parts(first, gp)
    second, down_a = lax.optimization_barrier((second, down_a))
    grad_a = lax.psum_scatter(down_a, "dp", scatter_dimension=0, tiled=True)

    mate_second = swap(second)
    h, rows = hidden(second, wd, u_a, c1, c2, p, width)
    h_mate = swap(h)
    parts = units(me, first, mate_first, second, mate_second, h, h_mate, gp, gp_mate)
    parts, grad_a, rows = lax.optimization_barrier((parts, grad_a, rows))
    sums = lax.psum_scatter(parts, "dp", scatter_dimension=0, tiled=True, axis_index_groups=CHIPS)
    back = exchange(input_rows(h, w, 0, width, rows))

    gate_up_grad = sums[:SLICE].reshape(SLICE, 2, 1, ff)
    down_grad = jnp.concatenate([grad_a, sums[SLICE:, :ff], sums[SLICE:, ff:]], axis=0)[:, None, :]
    input_grad, gate_grad = unpack(hot, ids, back, width)
    return (input_grad, gate_grad.T, gate_up_grad, down_grad)


def solution(mesh):
    placed = (
        P(("dp", "expert"), None),
        P(("dp", "expert"), None),
        P(("dp", "expert"), None),
        P(("dp", "expert"), None),
        P(None, None, "expert", None),
        P(None, "expert", None),
    )
    return jax.shard_map(
        body,
        mesh=mesh,
        in_specs=placed,
        out_specs=(
            P(("dp", "expert"), None),
            P(("dp", "expert"), None),
            P("dp", None, "expert", None),
            P("dp", "expert", None),
        ),
        check_vma=False,
    )
```

```python
import functools

import jax
import jax.numpy as jnp
from jax import lax
from jax.experimental import pallas as pl
from jax.experimental.pallas import tpu as pltpu
from jax.sharding import PartitionSpec as P

BF = jnp.bfloat16
F32 = jnp.float32
SLICE = 512
PART_A = 256
PART_B = SLICE - PART_A
SLICES = 8
GRADS = SLICES * SLICE
FIRST = GRADS + SLICES * PART_A
CAP = 32
LANES = 128
PACK_STEPS = 2
PRE_PER = 2
INPUT_BLOCK = 1024


def params(mib):
    return pltpu.CompilerParams(vmem_limit_bytes=mib * 1024 * 1024)


def in_hbm(x):
    return pltpu.with_memory_space_constraint(x, pltpu.HBM)


def in_vmem(x):
    return pltpu.with_memory_space_constraint(x, pltpu.VMEM)


def held(shape):
    return pl.BlockSpec(shape, lambda *_: (0,) * len(shape), pipeline_mode=pl.Buffered(1))


def left_in_hbm():
    return pl.BlockSpec(memory_space=pltpu.HBM)


def dot_nn(a, b):
    return lax.dot_general(a, b, (((1,), (0,)), ((), ())), preferred_element_type=F32)


def dot_nt(a, b):
    return lax.dot_general(a, b, (((1,), (1,)), ((), ())), preferred_element_type=F32)


def dot_tn(a, b):
    return lax.dot_general(a, b, (((0,), (0,)), ((), ())), preferred_element_type=F32)


def pack_kernel(ids_ref, gates_ref, tok_ref, dy_ref, first_ref, second_ref, hot_ref, *, step_experts):
    tokens = ids_ref.shape[1]
    base = pl.program_id(0) * step_experts
    expert = lax.broadcasted_iota(jnp.int32, (8, tokens), 0) + base
    zero = jnp.zeros((8, tokens), F32)
    is_0 = ids_ref[0:1, :] == expert
    is_1 = ids_ref[1:2, :] == expert
    named = is_0 | is_1
    member = jnp.where(named, 1.0, 0.0).astype(BF)
    row = lax.broadcasted_iota(jnp.int32, (tokens, tokens), 0)
    col = lax.broadcasted_iota(jnp.int32, (tokens, tokens), 1)
    earlier = jnp.where(row < col, 1.0, 0.0).astype(BF)
    place = jnp.where(named, dot_nn(member, earlier), -1.0)
    gates = gates_ref[...].astype(F32)
    weight = jnp.where(is_0, gates[0:1, :], zero) + jnp.where(is_1, gates[1:2, :], zero)
    rows = step_experts * CAP
    place_all = jnp.broadcast_to(place[:step_experts, None, :], (step_experts, CAP, tokens)).reshape(rows, tokens)
    weight_all = jnp.broadcast_to(weight[:step_experts, None, :], (step_experts, CAP, tokens)).reshape(rows, tokens)
    slot = (lax.broadcasted_iota(jnp.int32, (rows, tokens), 0) % CAP).astype(F32)
    hot = jnp.where(place_all == slot, 1.0, 0.0)
    slot_gate = jnp.sum(hot * weight_all, axis=1, keepdims=True)
    first_ref[:, FIRST:] = jnp.broadcast_to(slot_gate, (rows, LANES)).astype(BF)
    hot = hot.astype(BF)
    hot_ref[...] = hot
    for q in range(SLICES):
        cols = slice(q * SLICE, (q + 1) * SLICE)
        first_ref[:, cols] = dot_nn(hot, tok_ref[:, cols]).astype(BF)
        grads = dot_nn(hot, dy_ref[:, cols]).astype(BF)
        first_ref[:, GRADS + q * PART_A : GRADS + (q + 1) * PART_A] = grads[:, :PART_A]
        second_ref[:, q * PART_B : (q + 1) * PART_B] = grads[:, PART_A:]


def pack(ids, gates, tokens_in, out_grad, slots):
    steps = PACK_STEPS
    tok_dev, width = tokens_in.shape
    rows = slots // steps
    wide = FIRST + LANES
    whole = lambda shape: pl.BlockSpec(shape, lambda i: (0, 0))
    return pl.pallas_call(
        functools.partial(pack_kernel, step_experts=rows // CAP),
        grid=(steps,),
        in_specs=[whole((2, tok_dev)), whole((2, tok_dev)), whole((tok_dev, width)), whole((tok_dev, width))],
        out_specs=[
            pl.BlockSpec((rows, wide), lambda i: (i, 0)),
            pl.BlockSpec((rows, SLICES * PART_B), lambda i: (i, 0)),
            pl.BlockSpec((rows, tok_dev), lambda i: (i, 0)),
        ],
        out_shape=[
            pltpu.HBM((slots, wide), BF),
            pltpu.HBM((slots, SLICES * PART_B), BF),
            pltpu.HBM((slots, tok_dev), BF),
        ],
        compiler_params=params(24),
        name="pack",
        cost_estimate=pl.CostEstimate(flops=3000000000, transcendentals=0, bytes_accessed=14000000),
    )(in_hbm(ids), in_hbm(gates), in_hbm(tokens_in), in_hbm(out_grad))


def pre_kernel(rows_ref, dy_ref, gate_ref, w_ref, wd_ref, *refs, per):
    outs, (u_acc, pg_acc, pu_acc, p_buf, gp_buf, sems) = refs[:5], refs[5:]
    step = pl.program_id(0)

    @pl.when(step == 0)
    def _():
        pg_acc[...] = jnp.zeros_like(pg_acc)
        pu_acc[...] = jnp.zeros_like(pu_acc)
        u_acc[...] = jnp.zeros_like(u_acc)

    depth = pl.ds(pl.multiple_of(step * per * SLICE, SLICE), per * SLICE)
    u_acc[...] += dot_nn(dy_ref[...], wd_ref[...].reshape(per * PART_A, wd_ref.shape[3]))
    x = rows_ref[...]
    pg_acc[...] += dot_nn(x, w_ref[0, depth, :])
    pu_acc[...] += dot_nn(x, w_ref[1, depth, :])

    @pl.when(step == pl.num_programs(0) - 1)
    def _():
        slots = pg_acc.shape[0]
        chunk, part = 32, slots // 4
        copies = [pltpu.make_async_copy(u_acc, outs[0], sems.at[4, 0])]
        copies[0].start()
        for k in range(4):

            def one(i, carry):
                at = pl.ds(pl.multiple_of(k * part + i * chunk, chunk), chunk)
                pg = pg_acc[at, :]
                pu = pu_acc[at, :]
                g = gate_ref[at, :].astype(F32)[:, :1]
                s = jax.nn.sigmoid(pg)
                a = pg * s
                product = a * pu
                p_buf[at, :] = product.astype(BF)
                gp_buf[at, :] = (g * product).astype(BF)
                pg_acc[at, :] = g * (pu * s * (1.0 + pg * (1.0 - s)))
                pu_acc[at, :] = g * a
                return carry

            lax.fori_loop(0, part // chunk, one, 0)
            for j, (buf, out) in enumerate(zip((pg_acc, pu_acc, p_buf, gp_buf), outs[1:])):
                at = pl.ds(k * part, part)
                copies.append(pltpu.make_async_copy(buf.at[at], out.at[at], sems.at[j, k]))
                copies[-1].start()
        for copy in copies:
            copy.wait()


def pre(first, w, wd):
    slots = first.shape[0]
    ff = wd.shape[3]
    per = PRE_PER
    return pl.pallas_call(
        functools.partial(pre_kernel, per=per),
        grid=(SLICES // per,),
        in_specs=[
            pl.BlockSpec((slots, per * SLICE), lambda q: (0, q)),
            pl.BlockSpec((slots, per * PART_A), lambda q: (0, GRADS // (per * PART_A) + q)),
            pl.BlockSpec((slots, LANES), lambda q: (0, FIRST // LANES)),
            pl.BlockSpec(memory_space=pltpu.VMEM),
            pl.BlockSpec((per, 1, PART_A, ff), lambda q: (q, 0, 0, 0)),
        ],
        out_specs=[left_in_hbm()] * 5,
        out_shape=[pltpu.HBM((slots, ff), t) for t in (F32, F32, F32, BF, BF)],
        scratch_shapes=[pltpu.VMEM((slots, ff), t) for t in (F32, F32, F32, BF, BF)]
        + [pltpu.SemaphoreType.DMA((5, 4))],
        compiler_params=params(24),
        name="pre",
        cost_estimate=pl.CostEstimate(flops=17000000000, transcendentals=0, bytes_accessed=40000000),
    )(in_hbm(first), in_hbm(first), in_hbm(first), in_vmem(w), in_hbm(wd))


def hidden_kernel(dy_hbm, wd_hbm, u_hbm, c1_hbm, c2_hbm, p_hbm, h_ref, gate_ref, *scratch):
    dy, wd, u_acc, c1, c2, p, gate_acc, sems = scratch
    half = SLICES // 2
    depth = half * PART_B
    wanted = [
        (dy_hbm, dy),
        (wd_hbm.at[:half, 1], wd.at[:half]),
        (wd_hbm.at[half:, 1], wd.at[half:]),
        (u_hbm, u_acc),
        (c1_hbm, c1),
        (c2_hbm, c2),
        (p_hbm, p),
    ]
    copies = [pltpu.make_async_copy(src, dst, sems.at[k]) for k, (src, dst) in enumerate(wanted)]
    for copy in copies:
        copy.start()
    copies[0].wait()
    copies[1].wait()
    copies[3].wait()
    u_acc[...] += dot_nn(dy[:, :depth], wd[:half].reshape(depth, wd.shape[2]))
    copies[2].wait()
    u_acc[...] += dot_nn(dy[:, depth:], wd[half:].reshape(depth, wd.shape[2]))
    for copy in copies[4:]:
        copy.wait()
    chunk = 32

    def one(i, carry):
        at = pl.ds(pl.multiple_of(i * chunk, chunk), chunk)
        u = u_acc[at, :]
        h_ref[0, at, :] = (u * c1[at, :]).astype(BF)
        h_ref[1, at, :] = (u * c2[at, :]).astype(BF)
        both = u * p[at, :].astype(F32)
        folded = both[:, :LANES]
        for k in range(1, both.shape[1] // LANES):
            folded += both[:, k * LANES : (k + 1) * LANES]
        gate_acc[at, :] = folded
        return carry

    lax.fori_loop(0, u_acc.shape[0] // chunk, one, 0)
    total = jnp.sum(gate_acc[...], axis=1, keepdims=True)
    gate_ref[...] = jnp.broadcast_to(total, gate_ref.shape).astype(BF)


def hidden(second, wd, u_a, c1, c2, p, gate_at):
    slots, ff = p.shape
    return pl.pallas_call(
        hidden_kernel,
        grid=(1,),
        in_specs=[pl.BlockSpec(memory_space=pl.ANY)] + [left_in_hbm()] * 5,
        out_specs=[held((2, slots, ff)), pl.BlockSpec((slots, LANES), lambda j: (0, gate_at // LANES))],
        out_shape=[pltpu.HBM((2, slots, ff), BF), pltpu.HBM((slots, gate_at + LANES), BF)],
        scratch_shapes=[
            pltpu.VMEM(second.shape, BF),
            pltpu.VMEM((SLICES, PART_B, ff), BF),
            pltpu.VMEM((slots, ff), F32),
            pltpu.VMEM((slots, ff), F32),
            pltpu.VMEM((slots, ff), F32),
            pltpu.VMEM((slots, ff), BF),
            pltpu.VMEM((slots, LANES), F32),
            pltpu.SemaphoreType.DMA((7,)),
        ],
        compiler_params=params(24),
        name="hidden",
        cost_estimate=pl.CostEstimate(flops=4000000000, transcendentals=0, bytes_accessed=14000000),
    )(second, *map(in_hbm, (wd, u_a, c1, c2, p)))


def input_kernel(h_ref, w_ref, into_ref, out_ref):
    del into_ref
    out_ref[...] = (dot_nt(h_ref[0], w_ref[0]) + dot_nt(h_ref[1], w_ref[1])).astype(BF)


def input_rows(h, w, begin, cols, into):
    _, slots, ff = h.shape
    blk = INPUT_BLOCK
    first = begin // blk
    return pl.pallas_call(
        input_kernel,
        grid=(cols // blk,),
        in_specs=[held((2, slots, ff)), pl.BlockSpec((2, blk, ff), lambda j: (0, first + j, 0)), left_in_hbm()],
        out_specs=pl.BlockSpec((slots, blk), lambda j: (0, first + j)),
        out_shape=pltpu.HBM(into.shape, BF),
        input_output_aliases={2: 0},
        compiler_params=params(24),
        name="input_rows",
        cost_estimate=pl.CostEstimate(flops=13000000000, transcendentals=0, bytes_accessed=24000000),
    )(in_hbm(h), in_hbm(w), in_hbm(into))


def chip_at(me, hop, up):
    return jnp.where(up, me // 2 + 3 - hop, me // 2 + 1 + hop) % 4


def down_kernel(me_ref, own_ref, mate_ref, gp_ref, gp_mate_ref, up_ref, dn_ref, up_rest_ref, dn_rest_ref):
    del me_ref
    step = pl.program_id(0)
    part = (dot_tn(own_ref[...], gp_ref[...]) + dot_tn(mate_ref[...], gp_mate_ref[...])).astype(BF)
    half = PART_A // 2

    @pl.when(step == 0)
    def _():
        up_ref[...] = part[:half]

    @pl.when(step == 2)
    def _():
        dn_ref[...] = part[half:]

    up_rest_ref[0] = part[:half]
    dn_rest_ref[0] = part[half:]


def down_parts(me, own, mate, gp, gp_mate):
    slots, ff = gp.shape
    rows = pl.BlockSpec(
        (slots, PART_A), lambda i, me: (0, GRADS // PART_A + 2 * chip_at(me[0], i, True) + me[0] % 2)
    )
    half = PART_A // 2
    return pl.pallas_call(
        down_kernel,
        grid_spec=pltpu.PrefetchScalarGridSpec(
            num_scalar_prefetch=1,
            grid=(4,),
            in_specs=[rows, rows, held((slots, ff)), held((slots, ff))],
            out_specs=[pl.BlockSpec((half, ff), lambda i, me: (0, 0))] * 2
            + [pl.BlockSpec((1, half, ff), lambda i, me: (i, 0, 0))] * 2,
        ),
        out_shape=[pltpu.HBM((half, ff), BF)] * 2 + [pltpu.HBM((4, half, ff), BF)] * 2,
        compiler_params=params(16),
        name="down_parts",
        cost_estimate=pl.CostEstimate(flops=4000000000, transcendentals=0, bytes_accessed=12000000),
    )(me, in_hbm(own), in_hbm(mate), in_hbm(gp), gp_mate)


UNIT = SLICE // 2
EXTRA = PART_B // 4


def unit_part(own_ref, mate_ref, dy_ref, dy_mate_ref, h_ref, h_mate_ref, gp_ref, gp_mate_ref, out_ref):
    ff = gp_ref.shape[1]
    own = own_ref[...]
    mate = mate_ref[...]
    for k in range(2):
        part = dot_tn(own, h_ref[k]) + dot_tn(mate, h_mate_ref[k])
        out_ref[:UNIT, k * ff : (k + 1) * ff] = part.astype(BF)
    down = (dot_tn(dy_ref[...], gp_ref[...]) + dot_tn(dy_mate_ref[...], gp_mate_ref[...])).astype(BF)
    out_ref[UNIT:, :ff] = down[:EXTRA]
    out_ref[UNIT:, ff:] = down[EXTRA:]


def units_kernel(me_ref, *refs):
    del me_ref
    ins, outs = refs[:8], refs[8:]
    for k, out in enumerate(outs):

        @pl.when(pl.program_id(0) == k)
        def _():
            unit_part(*ins, out)


def units(me, first, mate_first, second, mate_second, h, h_mate, gp, gp_mate, hop, hops):
    _, slots, ff = h.shape
    at = lambda i, me: 2 * (2 * chip_at(me[0], hop + i // 2, i % 2 == 0) + me[0] % 2) + i % 2
    rows = pl.BlockSpec((slots, UNIT), lambda i, me: (0, at(i, me)))
    grads = pl.BlockSpec((slots, PART_B // 2), lambda i, me: (0, at(i, me)))
    shape = (UNIT + EXTRA, 2 * ff)
    return pl.pallas_call(
        units_kernel,
        grid_spec=pltpu.PrefetchScalarGridSpec(
            num_scalar_prefetch=1,
            grid=(2 * hops,),
            in_specs=[rows, rows, grads, grads] + [held((2, slots, ff))] * 2 + [held((slots, ff))] * 2,
            out_specs=[pl.BlockSpec(shape, lambda i, me: (0, 0))] * (2 * hops),
        ),
        out_shape=[pltpu.HBM(shape, BF)] * (2 * hops),
        compiler_params=params(28),
        name="units",
        cost_estimate=pl.CostEstimate(flops=4000000000, transcendentals=0, bytes_accessed=12000000),
    )(me, in_hbm(first), in_hbm(mate_first), second, mate_second, in_hbm(h), h_mate, in_hbm(gp), gp_mate)


def unpack_kernel(hot_ref, rows_ref, ids_ref, gates_ref, out_ref, gate_ref):
    out_ref[...] = dot_tn(hot_ref[...], rows_ref[...]).astype(BF)

    @pl.when(pl.program_id(0) == 0)
    def _():
        hot = hot_ref[...]
        expert = lax.broadcasted_iota(jnp.int32, hot.shape, 0) // CAP
        for k in range(2):
            chosen = jnp.where(expert == ids_ref[k : k + 1, :], hot.astype(F32), 0.0).astype(BF)
            gate_ref[k : k + 1, :] = dot_tn(gates_ref[...], chosen)[0:1, :].astype(BF)


def unpack(hot, ids, back, width):
    slots, tok_dev = hot.shape
    blk = 1024
    whole = lambda shape: pl.BlockSpec(shape, lambda i: (0, 0))
    return pl.pallas_call(
        unpack_kernel,
        grid=(width // blk,),
        in_specs=[
            whole((slots, tok_dev)),
            pl.BlockSpec((slots, blk), lambda i: (0, i)),
            whole((2, tok_dev)),
            pl.BlockSpec((slots, LANES), lambda i: (0, width // LANES)),
        ],
        out_specs=[pl.BlockSpec((tok_dev, blk), lambda i: (0, i)), whole((2, tok_dev))],
        out_shape=[pltpu.HBM((tok_dev, width), BF), pltpu.HBM((2, tok_dev), BF)],
        compiler_params=params(16),
        name="unpack",
        cost_estimate=pl.CostEstimate(flops=1000000000, transcendentals=0, bytes_accessed=10000000),
    )(*map(in_hbm, (hot, back, ids, back)))


SWAP = [(i, i ^ 1) for i in range(8)]
UP = [(i, (i + 2) % 8) for i in range(8)]
DOWN = [(i, (i - 2) % 8) for i in range(8)]


def pass_on(up, dn):
    return lax.ppermute(up, "dp", UP), lax.ppermute(dn, "dp", DOWN)


def added(arrived, parts):
    return tuple((a.astype(F32) + b.astype(F32)).astype(BF) for a, b in zip(arrived, parts))


def body(tokens_in, out_grad, expert_ids, gate_probs, gate_up, down_proj):
    width = tokens_in.shape[1]
    owners = lax.axis_size("expert")
    ff = gate_up.shape[3]
    slots = owners * CAP
    me = lax.axis_index("dp")

    ids = expert_ids.T
    first, second, hot = pack(ids, gate_probs.T, tokens_in, out_grad, slots)

    def exchange(rows):
        wide = rows.shape[1]
        got = lax.all_to_all(rows.reshape(owners, CAP, wide), "expert", split_axis=0, concat_axis=0, tiled=True)
        return got.reshape(slots, wide)

    def swap(x):
        return lax.ppermute(x, "dp", SWAP)

    me = me.reshape(1).astype(jnp.int32)
    first, me = lax.optimization_barrier((first, me))
    first, gate_up, down_proj = lax.optimization_barrier((exchange(first), gate_up, down_proj))
    second = exchange(second)
    mate_first = swap(first)
    w = jnp.transpose(gate_up[:, :, 0], (1, 0, 2))
    wd = down_proj.reshape(SLICES, 2, PART_A, ff)
    u_a, c1, c2, p, gp = pre(first, w, wd)
    gp_mate = swap(gp)
    down_up, down_dn, rest_up, rest_dn = down_parts(me, first, mate_first, gp, gp_mate)
    down_sum = pass_on(down_up, down_dn)
    second, rest_up, rest_dn = lax.optimization_barrier((second, rest_up, rest_dn))
    mate_second = swap(second)
    h, rows = hidden(second, wd, u_a, c1, c2, p, width)
    h_mate = swap(h)
    h_mate, down_sum = lax.optimization_barrier((h_mate, down_sum))
    args = (me, first, mate_first, second, mate_second)
    total = units(*args, h, h_mate, gp, gp_mate, 0, 1)
    down_sum = pass_on(*added(down_sum, (rest_up[1], rest_dn[1])))
    h, total = lax.optimization_barrier((h, total))
    total = pass_on(*total)
    rows = input_rows(h, w, 0, width, rows)
    h, rows, down_sum = lax.optimization_barrier((h, rows, down_sum))
    back = exchange(rows)
    parts = units(*args, h, h_mate, gp, gp_mate, 1, 1)
    down_sum = pass_on(*added(down_sum, (rest_up[2], rest_dn[0])))
    total = added(total, parts)
    h, total = lax.optimization_barrier((h, total))
    total = pass_on(*total)
    parts = units(*args, h, h_mate, gp, gp_mate, 2, 2)
    total, down_sum = lax.optimization_barrier((total, down_sum))
    total = pass_on(*added(total, parts[:2]))
    total, back = lax.optimization_barrier((total, back))
    down_sum = added(down_sum, (rest_up[3], rest_dn[3]))
    sum_up, sum_dn = added(total, parts[2:])

    sums = jnp.concatenate([sum_up[:UNIT], sum_dn[:UNIT]], axis=0)
    gate_up_grad = sums.reshape(SLICE, 2, 1, ff)
    down_b = [t[UNIT:, k * ff : (k + 1) * ff] for t in (sum_up, sum_dn) for k in range(2)]
    down_grad = jnp.concatenate(list(down_sum) + down_b, axis=0)[:, None, :]
    input_grad, gate_grad = unpack(hot, ids, back, width)
    return (input_grad, gate_grad.T, gate_up_grad, down_grad)


def solution(mesh):
    placed = (
        P(("dp", "expert"), None),
        P(("dp", "expert"), None),
        P(("dp", "expert"), None),
        P(("dp", "expert"), None),
        P(None, None, "expert", None),
        P(None, "expert", None),
    )
    return jax.shard_map(
        body,
        mesh=mesh,
        in_specs=placed,
        out_specs=(
            P(("dp", "expert"), None),
            P(("dp", "expert"), None),
            P("dp", None, "expert", None),
            P("dp", "expert", None),
        ),
        check_vma=False,
    )
```

```python
import functools

import jax
import jax.numpy as jnp
from jax import lax
from jax.experimental import pallas as pl
from jax.experimental.pallas import tpu as pltpu
from jax.sharding import PartitionSpec as P

BF = jnp.bfloat16
F32 = jnp.float32
SLICE = 512
PART_A = 256
PART_B = SLICE - PART_A
SLICES = 8
GRADS = SLICES * SLICE
FIRST = GRADS + SLICES * PART_A
CAP = 32
LANES = 128
PACK_STEPS = 2
PRE_PER = 2
INPUT_BLOCK = 1024


def params(mib):
    return pltpu.CompilerParams(vmem_limit_bytes=mib * 1024 * 1024)


def in_hbm(x):
    return pltpu.with_memory_space_constraint(x, pltpu.HBM)


def in_vmem(x):
    return pltpu.with_memory_space_constraint(x, pltpu.VMEM)


def held(shape):
    return pl.BlockSpec(shape, lambda *_: (0,) * len(shape), pipeline_mode=pl.Buffered(1))


def left_in_hbm():
    return pl.BlockSpec(memory_space=pltpu.HBM)


def dot_nn(a, b):
    return lax.dot_general(a, b, (((1,), (0,)), ((), ())), preferred_element_type=F32)


def dot_nt(a, b):
    return lax.dot_general(a, b, (((1,), (1,)), ((), ())), preferred_element_type=F32)


def dot_tn(a, b):
    return lax.dot_general(a, b, (((0,), (0,)), ((), ())), preferred_element_type=F32)


def pack_kernel(ids_ref, gates_ref, tok_ref, dy_ref, first_ref, second_ref, hot_ref, *, step_experts):
    tokens = ids_ref.shape[1]
    base = pl.program_id(0) * step_experts
    expert = lax.broadcasted_iota(jnp.int32, (8, tokens), 0) + base
    zero = jnp.zeros((8, tokens), F32)
    is_0 = ids_ref[0:1, :] == expert
    is_1 = ids_ref[1:2, :] == expert
    named = is_0 | is_1
    member = jnp.where(named, 1.0, 0.0).astype(BF)
    row = lax.broadcasted_iota(jnp.int32, (tokens, tokens), 0)
    col = lax.broadcasted_iota(jnp.int32, (tokens, tokens), 1)
    earlier = jnp.where(row < col, 1.0, 0.0).astype(BF)
    place = jnp.where(named, dot_nn(member, earlier), -1.0)
    gates = gates_ref[...].astype(F32)
    weight = jnp.where(is_0, gates[0:1, :], zero) + jnp.where(is_1, gates[1:2, :], zero)
    rows = step_experts * CAP
    place_all = jnp.broadcast_to(place[:step_experts, None, :], (step_experts, CAP, tokens)).reshape(rows, tokens)
    weight_all = jnp.broadcast_to(weight[:step_experts, None, :], (step_experts, CAP, tokens)).reshape(rows, tokens)
    slot = (lax.broadcasted_iota(jnp.int32, (rows, tokens), 0) % CAP).astype(F32)
    hot = jnp.where(place_all == slot, 1.0, 0.0)
    slot_gate = jnp.sum(hot * weight_all, axis=1, keepdims=True)
    first_ref[:, FIRST:] = jnp.broadcast_to(slot_gate, (rows, LANES)).astype(BF)
    hot = hot.astype(BF)
    hot_ref[...] = hot
    for q in range(SLICES):
        cols = slice(q * SLICE, (q + 1) * SLICE)
        first_ref[:, cols] = dot_nn(hot, tok_ref[:, cols]).astype(BF)
        grads = dot_nn(hot, dy_ref[:, cols]).astype(BF)
        first_ref[:, GRADS + q * PART_A : GRADS + (q + 1) * PART_A] = grads[:, :PART_A]
        second_ref[:, q * PART_B : (q + 1) * PART_B] = grads[:, PART_A:]


def pack(ids, gates, tokens_in, out_grad, slots):
    steps = PACK_STEPS
    tok_dev, width = tokens_in.shape
    rows = slots // steps
    wide = FIRST + LANES
    whole = lambda shape: pl.BlockSpec(shape, lambda i: (0, 0))
    return pl.pallas_call(
        functools.partial(pack_kernel, step_experts=rows // CAP),
        grid=(steps,),
        in_specs=[whole((2, tok_dev)), whole((2, tok_dev)), whole((tok_dev, width)), whole((tok_dev, width))],
        out_specs=[
            pl.BlockSpec((rows, wide), lambda i: (i, 0)),
            pl.BlockSpec((rows, SLICES * PART_B), lambda i: (i, 0)),
            pl.BlockSpec((rows, tok_dev), lambda i: (i, 0)),
        ],
        out_shape=[
            pltpu.HBM((slots, wide), BF),
            pltpu.HBM((slots, SLICES * PART_B), BF),
            pltpu.HBM((slots, tok_dev), BF),
        ],
        compiler_params=params(24),
        name="pack",
        cost_estimate=pl.CostEstimate(flops=3000000000, transcendentals=0, bytes_accessed=14000000),
    )(in_hbm(ids), in_hbm(gates), in_hbm(tokens_in), in_hbm(out_grad))


def pre_kernel(rows_ref, dy_ref, gate_ref, w_ref, wd_ref, *refs, per):
    outs, (u_acc, pg_acc, pu_acc, p_buf, gp_buf, sems) = refs[:5], refs[5:]
    step = pl.program_id(0)

    @pl.when(step == 0)
    def _():
        pg_acc[...] = jnp.zeros_like(pg_acc)
        pu_acc[...] = jnp.zeros_like(pu_acc)
        u_acc[...] = jnp.zeros_like(u_acc)

    depth = pl.ds(pl.multiple_of(step * per * SLICE, SLICE), per * SLICE)
    u_acc[...] += dot_nn(dy_ref[...], wd_ref[...].reshape(per * PART_A, wd_ref.shape[3]))
    x = rows_ref[...]
    pg_acc[...] += dot_nn(x, w_ref[0, depth, :])
    pu_acc[...] += dot_nn(x, w_ref[1, depth, :])

    @pl.when(step == pl.num_programs(0) - 1)
    def _():
        slots = pg_acc.shape[0]
        chunk, part = 32, slots // 4
        copies = [pltpu.make_async_copy(u_acc, outs[0], sems.at[4, 0])]
        copies[0].start()
        for k in range(4):

            def one(i, carry):
                at = pl.ds(pl.multiple_of(k * part + i * chunk, chunk), chunk)
                pg = pg_acc[at, :]
                pu = pu_acc[at, :]
                g = gate_ref[at, :].astype(F32)[:, :1]
                s = jax.nn.sigmoid(pg)
                a = pg * s
                product = a * pu
                p_buf[at, :] = product.astype(BF)
                gp_buf[at, :] = (g * product).astype(BF)
                pg_acc[at, :] = g * (pu * s * (1.0 + pg * (1.0 - s)))
                pu_acc[at, :] = g * a
                return carry

            lax.fori_loop(0, part // chunk, one, 0)
            for j, (buf, out) in enumerate(zip((pg_acc, pu_acc, p_buf, gp_buf), outs[1:])):
                at = pl.ds(k * part, part)
                copies.append(pltpu.make_async_copy(buf.at[at], out.at[at], sems.at[j, k]))
                copies[-1].start()
        for copy in copies:
            copy.wait()


def pre(first, w, wd):
    slots = first.shape[0]
    ff = wd.shape[3]
    per = PRE_PER
    return pl.pallas_call(
        functools.partial(pre_kernel, per=per),
        grid=(SLICES // per,),
        in_specs=[
            pl.BlockSpec((slots, per * SLICE), lambda q: (0, q)),
            pl.BlockSpec((slots, per * PART_A), lambda q: (0, GRADS // (per * PART_A) + q)),
            pl.BlockSpec((slots, LANES), lambda q: (0, FIRST // LANES)),
            pl.BlockSpec(memory_space=pltpu.VMEM),
            pl.BlockSpec((per, 1, PART_A, ff), lambda q: (q, 0, 0, 0)),
        ],
        out_specs=[left_in_hbm()] * 5,
        out_shape=[pltpu.HBM((slots, ff), t) for t in (F32, F32, F32, BF, BF)],
        scratch_shapes=[pltpu.VMEM((slots, ff), t) for t in (F32, F32, F32, BF, BF)]
        + [pltpu.SemaphoreType.DMA((5, 4))],
        compiler_params=params(24),
        name="pre",
        cost_estimate=pl.CostEstimate(flops=17000000000, transcendentals=0, bytes_accessed=40000000),
    )(in_hbm(first), in_hbm(first), in_hbm(first), in_vmem(w), in_hbm(wd))


def hidden_kernel(dy_hbm, wd_hbm, u_hbm, c1_hbm, c2_hbm, p_hbm, h_ref, gate_ref, *scratch):
    dy, wd, u_acc, c1, c2, p, gate_acc, sems = scratch
    half = SLICES // 2
    depth = half * PART_B
    wanted = [
        (dy_hbm, dy),
        (wd_hbm.at[:half, 1], wd.at[:half]),
        (wd_hbm.at[half:, 1], wd.at[half:]),
        (u_hbm, u_acc),
        (c1_hbm, c1),
        (c2_hbm, c2),
        (p_hbm, p),
    ]
    copies = [pltpu.make_async_copy(src, dst, sems.at[k]) for k, (src, dst) in enumerate(wanted)]
    for copy in copies:
        copy.start()
    copies[0].wait()
    copies[1].wait()
    copies[3].wait()
    u_acc[...] += dot_nn(dy[:, :depth], wd[:half].reshape(depth, wd.shape[2]))
    copies[2].wait()
    u_acc[...] += dot_nn(dy[:, depth:], wd[half:].reshape(depth, wd.shape[2]))
    for copy in copies[4:]:
        copy.wait()
    chunk = 32

    def one(i, carry):
        at = pl.ds(pl.multiple_of(i * chunk, chunk), chunk)
        u = u_acc[at, :]
        h_ref[0, at, :] = (u * c1[at, :]).astype(BF)
        h_ref[1, at, :] = (u * c2[at, :]).astype(BF)
        both = u * p[at, :].astype(F32)
        folded = both[:, :LANES]
        for k in range(1, both.shape[1] // LANES):
            folded += both[:, k * LANES : (k + 1) * LANES]
        gate_acc[at, :] = folded
        return carry

    lax.fori_loop(0, u_acc.shape[0] // chunk, one, 0)
    total = jnp.sum(gate_acc[...], axis=1, keepdims=True)
    gate_ref[...] = jnp.broadcast_to(total, gate_ref.shape).astype(BF)


def hidden(second, wd, u_a, c1, c2, p, gate_at):
    slots, ff = p.shape
    return pl.pallas_call(
        hidden_kernel,
        grid=(1,),
        in_specs=[pl.BlockSpec(memory_space=pl.ANY)] + [left_in_hbm()] * 5,
        out_specs=[held((2, slots, ff)), pl.BlockSpec((slots, LANES), lambda j: (0, gate_at // LANES))],
        out_shape=[pltpu.HBM((2, slots, ff), BF), pltpu.HBM((slots, gate_at + LANES), BF)],
        scratch_shapes=[
            pltpu.VMEM(second.shape, BF),
            pltpu.VMEM((SLICES, PART_B, ff), BF),
            pltpu.VMEM((slots, ff), F32),
            pltpu.VMEM((slots, ff), F32),
            pltpu.VMEM((slots, ff), F32),
            pltpu.VMEM((slots, ff), BF),
            pltpu.VMEM((slots, LANES), F32),
            pltpu.SemaphoreType.DMA((7,)),
        ],
        compiler_params=params(24),
        name="hidden",
        cost_estimate=pl.CostEstimate(flops=4000000000, transcendentals=0, bytes_accessed=14000000),
    )(second, *map(in_hbm, (wd, u_a, c1, c2, p)))


def input_kernel(h_ref, w_ref, into_ref, out_ref):
    del into_ref
    out_ref[...] = (dot_nt(h_ref[0], w_ref[0]) + dot_nt(h_ref[1], w_ref[1])).astype(BF)


def input_rows(h, w, begin, cols, into):
    _, slots, ff = h.shape
    blk = INPUT_BLOCK
    first = begin // blk
    return pl.pallas_call(
        input_kernel,
        grid=(cols // blk,),
        in_specs=[held((2, slots, ff)), pl.BlockSpec((2, blk, ff), lambda j: (0, first + j, 0)), left_in_hbm()],
        out_specs=pl.BlockSpec((slots, blk), lambda j: (0, first + j)),
        out_shape=pltpu.HBM(into.shape, BF),
        input_output_aliases={2: 0},
        compiler_params=params(24),
        name="input_rows",
        cost_estimate=pl.CostEstimate(flops=13000000000, transcendentals=0, bytes_accessed=24000000),
    )(in_hbm(h), in_hbm(w), in_hbm(into))


def chip_at(me, hop, up):
    return jnp.where(up, me // 2 + 3 - hop, me // 2 + 1 + hop) % 4


UNIT = SLICE // 2
EXTRA = UNIT // 2


def unit_part(own_ref, mate_ref, dy_ref, dy_mate_ref, h_ref, h_mate_ref, gp_ref, gp_mate_ref, out_ref):
    ff = gp_ref.shape[1]
    own = own_ref[...]
    mate = mate_ref[...]
    for k in range(2):
        part = dot_tn(own, h_ref[k]) + dot_tn(mate, h_mate_ref[k])
        out_ref[:UNIT, k * ff : (k + 1) * ff] = part.astype(BF)
    down = (dot_tn(dy_ref[...], gp_ref[...]) + dot_tn(dy_mate_ref[...], gp_mate_ref[...])).astype(BF)
    out_ref[UNIT:, :ff] = down[:EXTRA]
    out_ref[UNIT:, ff:] = down[EXTRA:]


def units_kernel(me_ref, *refs):
    del me_ref
    own, mate, dy_a, dy_a_mate, dy_b, dy_b_mate = refs[:6]
    hid, outs = refs[6:10], refs[10:]
    for k, out in enumerate(outs):

        @pl.when(pl.program_id(0) == k)
        def _():
            dy = (dy_a, dy_a_mate) if k % 2 == 0 else (dy_b, dy_b_mate)
            unit_part(own, mate, *dy, *hid, out)


def units(me, first, mate_first, second, mate_second, h, h_mate, gp, gp_mate, hop, hops):
    _, slots, ff = h.shape
    at = lambda i, me: 2 * chip_at(me[0], hop + i // 2, i % 2 == 0) + me[0] % 2
    rows = pl.BlockSpec((slots, UNIT), lambda i, me: (0, 2 * at(i, me) + i % 2))
    grads_a = pl.BlockSpec((slots, PART_A), lambda i, me: (0, GRADS // PART_A + at(i - i % 2, me)))
    grads_b = pl.BlockSpec((slots, PART_B), lambda i, me: (0, at(i - i % 2 + 1, me)))
    shape = (UNIT + EXTRA, 2 * ff)
    free = (lambda x: x) if hop == 0 else in_hbm
    return pl.pallas_call(
        units_kernel,
        grid_spec=pltpu.PrefetchScalarGridSpec(
            num_scalar_prefetch=1,
            grid=(2 * hops,),
            in_specs=[rows, rows, grads_a, grads_a, grads_b, grads_b]
            + [held((2, slots, ff))] * 2
            + [held((slots, ff))] * 2,
            out_specs=[pl.BlockSpec(shape, lambda i, me: (0, 0))] * (2 * hops),
        ),
        out_shape=[pltpu.HBM(shape, BF)] * (2 * hops),
        compiler_params=params(30),
        name="units",
        cost_estimate=pl.CostEstimate(flops=4000000000, transcendentals=0, bytes_accessed=12000000),
    )(
        me,
        *map(in_hbm, (first, mate_first, first, mate_first)),
        *map(free, (second, mate_second)),
        in_hbm(h),
        free(h_mate),
        in_hbm(gp),
        free(gp_mate),
    )


def unpack_kernel(hot_ref, rows_ref, ids_ref, gates_ref, out_ref, gate_ref):
    out_ref[...] = dot_tn(hot_ref[...], rows_ref[...]).astype(BF)

    @pl.when(pl.program_id(0) == 0)
    def _():
        hot = hot_ref[...]
        expert = lax.broadcasted_iota(jnp.int32, hot.shape, 0) // CAP
        for k in range(2):
            chosen = jnp.where(expert == ids_ref[k : k + 1, :], hot.astype(F32), 0.0).astype(BF)
            gate_ref[k : k + 1, :] = dot_tn(gates_ref[...], chosen)[0:1, :].astype(BF)


def unpack(hot, ids, back, width):
    slots, tok_dev = hot.shape
    blk = 1024
    whole = lambda shape: pl.BlockSpec(shape, lambda i: (0, 0))
    return pl.pallas_call(
        unpack_kernel,
        grid=(width // blk,),
        in_specs=[
            whole((slots, tok_dev)),
            pl.BlockSpec((slots, blk), lambda i: (0, i)),
            whole((2, tok_dev)),
            pl.BlockSpec((slots, LANES), lambda i: (0, width // LANES)),
        ],
        out_specs=[pl.BlockSpec((tok_dev, blk), lambda i: (0, i)), whole((2, tok_dev))],
        out_shape=[pltpu.HBM((tok_dev, width), BF), pltpu.HBM((2, tok_dev), BF)],
        compiler_params=params(16),
        name="unpack",
        cost_estimate=pl.CostEstimate(flops=1000000000, transcendentals=0, bytes_accessed=10000000),
    )(*map(in_hbm, (hot, back, ids, back)))


SWAP = [(i, i ^ 1) for i in range(8)]
UP = [(i, (i + 2) % 8) for i in range(8)]
DOWN = [(i, (i - 2) % 8) for i in range(8)]


def pass_on(up, dn):
    return lax.ppermute(up, "dp", UP), lax.ppermute(dn, "dp", DOWN)


def added(arrived, parts):
    return tuple((a.astype(F32) + b.astype(F32)).astype(BF) for a, b in zip(arrived, parts))


def body(tokens_in, out_grad, expert_ids, gate_probs, gate_up, down_proj):
    width = tokens_in.shape[1]
    owners = lax.axis_size("expert")
    ff = gate_up.shape[3]
    slots = owners * CAP
    me = lax.axis_index("dp")

    ids = expert_ids.T
    first, second, hot = pack(ids, gate_probs.T, tokens_in, out_grad, slots)

    def exchange(rows):
        wide = rows.shape[1]
        got = lax.all_to_all(rows.reshape(owners, CAP, wide), "expert", split_axis=0, concat_axis=0, tiled=True)
        return got.reshape(slots, wide)

    def swap(x):
        return lax.ppermute(x, "dp", SWAP)

    me = me.reshape(1).astype(jnp.int32)
    first, me = lax.optimization_barrier((first, me))
    first, gate_up, down_proj = lax.optimization_barrier((exchange(first), gate_up, down_proj))
    second = exchange(second)
    mate_first = swap(first)
    w = jnp.transpose(gate_up[:, :, 0], (1, 0, 2))
    wd = down_proj.reshape(SLICES, 2, PART_A, ff)
    u_a, c1, c2, p, gp = pre(first, w, wd)
    gp_mate = swap(gp)
    second, gp_mate = lax.optimization_barrier((second, gp_mate))
    mate_second = swap(second)
    h, rows = hidden(second, wd, u_a, c1, c2, p, width)
    h_mate = swap(h)
    args = (me, first, mate_first, second, mate_second)
    total = units(*args, h, h_mate, gp, gp_mate, 0, 1)
    h, total = lax.optimization_barrier((h, total))
    total = pass_on(*total)
    parts = units(*args, h, h_mate, gp, gp_mate, 1, 1)
    h, parts = lax.optimization_barrier((h, parts))
    rows = input_rows(h, w, 0, width, rows)
    h, rows = lax.optimization_barrier((h, rows))
    back = exchange(rows)
    total, rows = lax.optimization_barrier((total, rows))
    total = added(total, parts)
    h, total = lax.optimization_barrier((h, total))
    total = pass_on(*total)
    parts = units(*args, h, h_mate, gp, gp_mate, 2, 2)
    total = pass_on(*added(total, parts[:2]))
    input_grad, gate_grad = unpack(hot, ids, back, width)
    total, input_grad = lax.optimization_barrier((total, input_grad))
    sum_up, sum_dn = added(total, parts[2:])

    sums = jnp.concatenate([sum_up[:UNIT], sum_dn[:UNIT]], axis=0)
    gate_up_grad = sums.reshape(SLICE, 2, 1, ff)
    down = [t[UNIT:, k * ff : (k + 1) * ff] for t in (sum_up, sum_dn) for k in range(2)]
    down_grad = jnp.concatenate(down, axis=0)[:, None, :]
    return (input_grad, gate_grad.T, gate_up_grad, down_grad)


def solution(mesh):
    placed = (
        P(("dp", "expert"), None),
        P(("dp", "expert"), None),
        P(("dp", "expert"), None),
        P(("dp", "expert"), None),
        P(None, None, "expert", None),
        P(None, "expert", None),
    )
    return jax.shard_map(
        body,
        mesh=mesh,
        in_specs=placed,
        out_specs=(
            P(("dp", "expert"), None),
            P(("dp", "expert"), None),
            P("dp", None, "expert", None),
            P("dp", "expert", None),
        ),
        check_vma=False,
    )
```

```python
import functools

import jax
import jax.numpy as jnp
from jax import lax
from jax.experimental import pallas as pl
from jax.experimental.pallas import tpu as pltpu
from jax.sharding import PartitionSpec as P

BF = jnp.bfloat16
F32 = jnp.float32
SLICE = 512
PART_A = 256
PART_B = SLICE - PART_A
SLICES = 8
GRADS = SLICES * SLICE
FIRST = GRADS + SLICES * PART_A
CAP = 32
LANES = 128
PACK_STEPS = 2
PRE_PER = 2
INPUT_BLOCK = 1024


def params(mib):
    return pltpu.CompilerParams(vmem_limit_bytes=mib * 1024 * 1024)


def in_hbm(x):
    return pltpu.with_memory_space_constraint(x, pltpu.HBM)


def in_vmem(x):
    return pltpu.with_memory_space_constraint(x, pltpu.VMEM)


def held(shape):
    return pl.BlockSpec(shape, lambda *_: (0,) * len(shape), pipeline_mode=pl.Buffered(1))


def left_in_hbm():
    return pl.BlockSpec(memory_space=pltpu.HBM)


def dot_nn(a, b):
    return lax.dot_general(a, b, (((1,), (0,)), ((), ())), preferred_element_type=F32)


def dot_nt(a, b):
    return lax.dot_general(a, b, (((1,), (1,)), ((), ())), preferred_element_type=F32)


def dot_tn(a, b):
    return lax.dot_general(a, b, (((0,), (0,)), ((), ())), preferred_element_type=F32)


def pack_kernel(ids_ref, gates_ref, tok_ref, dy_ref, first_ref, second_ref, hot_ref, *, step_experts):
    tokens = ids_ref.shape[1]
    base = pl.program_id(0) * step_experts
    expert = lax.broadcasted_iota(jnp.int32, (8, tokens), 0) + base
    zero = jnp.zeros((8, tokens), F32)
    is_0 = ids_ref[0:1, :] == expert
    is_1 = ids_ref[1:2, :] == expert
    named = is_0 | is_1
    member = jnp.where(named, 1.0, 0.0).astype(BF)
    row = lax.broadcasted_iota(jnp.int32, (tokens, tokens), 0)
    col = lax.broadcasted_iota(jnp.int32, (tokens, tokens), 1)
    earlier = jnp.where(row < col, 1.0, 0.0).astype(BF)
    place = jnp.where(named, dot_nn(member, earlier), -1.0)
    gates = gates_ref[...].astype(F32)
    weight = jnp.where(is_0, gates[0:1, :], zero) + jnp.where(is_1, gates[1:2, :], zero)
    rows = step_experts * CAP
    place_all = jnp.broadcast_to(place[:step_experts, None, :], (step_experts, CAP, tokens)).reshape(rows, tokens)
    weight_all = jnp.broadcast_to(weight[:step_experts, None, :], (step_experts, CAP, tokens)).reshape(rows, tokens)
    slot = (lax.broadcasted_iota(jnp.int32, (rows, tokens), 0) % CAP).astype(F32)
    hot = jnp.where(place_all == slot, 1.0, 0.0)
    slot_gate = jnp.sum(hot * weight_all, axis=1, keepdims=True)
    first_ref[:, FIRST:] = jnp.broadcast_to(slot_gate, (rows, LANES)).astype(BF)
    hot = hot.astype(BF)
    hot_ref[...] = hot
    for q in range(SLICES):
        cols = slice(q * SLICE, (q + 1) * SLICE)
        first_ref[:, cols] = dot_nn(hot, tok_ref[:, cols]).astype(BF)
        grads = dot_nn(hot, dy_ref[:, cols]).astype(BF)
        first_ref[:, GRADS + q * PART_A : GRADS + (q + 1) * PART_A] = grads[:, :PART_A]
        second_ref[:, q * PART_B : (q + 1) * PART_B] = grads[:, PART_A:]


def pack(ids, gates, tokens_in, out_grad, slots):
    steps = PACK_STEPS
    tok_dev, width = tokens_in.shape
    rows = slots // steps
    wide = FIRST + LANES
    whole = lambda shape: pl.BlockSpec(shape, lambda i: (0, 0))
    return pl.pallas_call(
        functools.partial(pack_kernel, step_experts=rows // CAP),
        grid=(steps,),
        in_specs=[whole((2, tok_dev)), whole((2, tok_dev)), whole((tok_dev, width)), whole((tok_dev, width))],
        out_specs=[
            pl.BlockSpec((rows, wide), lambda i: (i, 0)),
            pl.BlockSpec((rows, SLICES * PART_B), lambda i: (i, 0)),
            pl.BlockSpec((rows, tok_dev), lambda i: (i, 0)),
        ],
        out_shape=[
            pltpu.HBM((slots, wide), BF),
            pltpu.HBM((slots, SLICES * PART_B), BF),
            pltpu.HBM((slots, tok_dev), BF),
        ],
        compiler_params=params(24),
        name="pack",
        cost_estimate=pl.CostEstimate(flops=3000000000, transcendentals=0, bytes_accessed=14000000),
    )(in_hbm(ids), in_hbm(gates), in_hbm(tokens_in), in_hbm(out_grad))


def pre_kernel(rows_ref, dy_ref, gate_ref, w_ref, wd_ref, *refs, per):
    outs, (u_acc, pg_acc, pu_acc, p_buf, gp_buf, sems) = refs[:5], refs[5:]
    step = pl.program_id(0)

    @pl.when(step == 0)
    def _():
        pg_acc[...] = jnp.zeros_like(pg_acc)
        pu_acc[...] = jnp.zeros_like(pu_acc)
        u_acc[...] = jnp.zeros_like(u_acc)

    depth = pl.ds(pl.multiple_of(step * per * SLICE, SLICE), per * SLICE)
    u_acc[...] += dot_nn(dy_ref[...], wd_ref[...].reshape(per * PART_A, wd_ref.shape[3]))
    x = rows_ref[...]
    pg_acc[...] += dot_nn(x, w_ref[0, depth, :])
    pu_acc[...] += dot_nn(x, w_ref[1, depth, :])

    @pl.when(step == pl.num_programs(0) - 1)
    def _():
        slots = pg_acc.shape[0]
        chunk, part = 32, slots // 4
        copies = [pltpu.make_async_copy(u_acc, outs[0], sems.at[4, 0])]
        copies[0].start()
        for k in range(4):

            def one(i, carry):
                at = pl.ds(pl.multiple_of(k * part + i * chunk, chunk), chunk)
                pg = pg_acc[at, :]
                pu = pu_acc[at, :]
                g = gate_ref[at, :].astype(F32)[:, :1]
                s = jax.nn.sigmoid(pg)
                a = pg * s
                product = a * pu
                p_buf[at, :] = product.astype(BF)
                gp_buf[at, :] = (g * product).astype(BF)
                pg_acc[at, :] = g * (pu * s * (1.0 + pg * (1.0 - s)))
                pu_acc[at, :] = g * a
                return carry

            lax.fori_loop(0, part // chunk, one, 0)
            for j, (buf, out) in enumerate(zip((pg_acc, pu_acc, p_buf, gp_buf), outs[1:])):
                at = pl.ds(k * part, part)
                copies.append(pltpu.make_async_copy(buf.at[at], out.at[at], sems.at[j, k]))
                copies[-1].start()
        for copy in copies:
            copy.wait()


def pre(first, w, wd):
    slots = first.shape[0]
    ff = wd.shape[3]
    per = PRE_PER
    return pl.pallas_call(
        functools.partial(pre_kernel, per=per),
        grid=(SLICES // per,),
        in_specs=[
            pl.BlockSpec((slots, per * SLICE), lambda q: (0, q)),
            pl.BlockSpec((slots, per * PART_A), lambda q: (0, GRADS // (per * PART_A) + q)),
            pl.BlockSpec((slots, LANES), lambda q: (0, FIRST // LANES)),
            pl.BlockSpec(memory_space=pltpu.VMEM),
            pl.BlockSpec((per, 1, PART_A, ff), lambda q: (q, 0, 0, 0)),
        ],
        out_specs=[left_in_hbm()] * 5,
        out_shape=[pltpu.HBM((slots, ff), t) for t in (F32, F32, F32, BF, BF)],
        scratch_shapes=[pltpu.VMEM((slots, ff), t) for t in (F32, F32, F32, BF, BF)]
        + [pltpu.SemaphoreType.DMA((5, 4))],
        compiler_params=params(24),
        name="pre",
        cost_estimate=pl.CostEstimate(flops=17000000000, transcendentals=0, bytes_accessed=40000000),
    )(in_hbm(first), in_hbm(first), in_hbm(first), in_vmem(w), in_hbm(wd))


def hidden_kernel(dy_hbm, wd_hbm, u_hbm, c1_hbm, c2_hbm, p_hbm, h_ref, gate_ref, *scratch):
    dy, wd, u_acc, c1, c2, p, gate_acc, sems = scratch
    half = SLICES // 2
    depth = half * PART_B
    wanted = [
        (dy_hbm, dy),
        (wd_hbm.at[:half, 1], wd.at[:half]),
        (wd_hbm.at[half:, 1], wd.at[half:]),
        (u_hbm, u_acc),
        (c1_hbm, c1),
        (c2_hbm, c2),
        (p_hbm, p),
    ]
    copies = [pltpu.make_async_copy(src, dst, sems.at[k]) for k, (src, dst) in enumerate(wanted)]
    for copy in copies:
        copy.start()
    copies[0].wait()
    copies[1].wait()
    copies[3].wait()
    u_acc[...] += dot_nn(dy[:, :depth], wd[:half].reshape(depth, wd.shape[2]))
    copies[2].wait()
    u_acc[...] += dot_nn(dy[:, depth:], wd[half:].reshape(depth, wd.shape[2]))
    for copy in copies[4:]:
        copy.wait()
    chunk = 32

    def one(i, carry):
        at = pl.ds(pl.multiple_of(i * chunk, chunk), chunk)
        u = u_acc[at, :]
        h_ref[0, at, :] = (u * c1[at, :]).astype(BF)
        h_ref[1, at, :] = (u * c2[at, :]).astype(BF)
        both = u * p[at, :].astype(F32)
        folded = both[:, :LANES]
        for k in range(1, both.shape[1] // LANES):
            folded += both[:, k * LANES : (k + 1) * LANES]
        gate_acc[at, :] = folded
        return carry

    lax.fori_loop(0, u_acc.shape[0] // chunk, one, 0)
    total = jnp.sum(gate_acc[...], axis=1, keepdims=True)
    gate_ref[...] = jnp.broadcast_to(total, gate_ref.shape).astype(BF)


def hidden(second, wd, u_a, c1, c2, p, gate_at):
    slots, ff = p.shape
    return pl.pallas_call(
        hidden_kernel,
        grid=(1,),
        in_specs=[pl.BlockSpec(memory_space=pl.ANY)] + [left_in_hbm()] * 5,
        out_specs=[held((2, slots, ff)), pl.BlockSpec((slots, LANES), lambda j: (0, gate_at // LANES))],
        out_shape=[pltpu.HBM((2, slots, ff), BF), pltpu.HBM((slots, gate_at + LANES), BF)],
        scratch_shapes=[
            pltpu.VMEM(second.shape, BF),
            pltpu.VMEM((SLICES, PART_B, ff), BF),
            pltpu.VMEM((slots, ff), F32),
            pltpu.VMEM((slots, ff), F32),
            pltpu.VMEM((slots, ff), F32),
            pltpu.VMEM((slots, ff), BF),
            pltpu.VMEM((slots, LANES), F32),
            pltpu.SemaphoreType.DMA((7,)),
        ],
        compiler_params=params(24),
        name="hidden",
        cost_estimate=pl.CostEstimate(flops=4000000000, transcendentals=0, bytes_accessed=14000000),
    )(second, *map(in_hbm, (wd, u_a, c1, c2, p)))


def input_kernel(h_ref, w_ref, into_ref, out_ref):
    del into_ref
    out_ref[...] = (dot_nt(h_ref[0], w_ref[0]) + dot_nt(h_ref[1], w_ref[1])).astype(BF)


def input_rows(h, w, begin, cols, into):
    _, slots, ff = h.shape
    blk = INPUT_BLOCK
    first = begin // blk
    return pl.pallas_call(
        input_kernel,
        grid=(cols // blk,),
        in_specs=[held((2, slots, ff)), pl.BlockSpec((2, blk, ff), lambda j: (0, first + j, 0)), left_in_hbm()],
        out_specs=pl.BlockSpec((slots, blk), lambda j: (0, first + j)),
        out_shape=pltpu.HBM(into.shape, BF),
        input_output_aliases={2: 0},
        compiler_params=params(24),
        name="input_rows",
        cost_estimate=pl.CostEstimate(flops=13000000000, transcendentals=0, bytes_accessed=24000000),
    )(in_hbm(h), in_hbm(w), in_hbm(into))


def chip_at(me, hop, up):
    return jnp.where(up, me // 2 + 3 - hop, me // 2 + 1 + hop) % 4


UNIT = SLICE // 2
EXTRA = UNIT // 2


def unit_part(own_ref, mate_ref, dy_ref, dy_mate_ref, h_ref, h_mate_ref, gp_ref, gp_mate_ref, out_ref):
    ff = gp_ref.shape[1]
    own = own_ref[...]
    mate = mate_ref[...]
    for k in range(2):
        part = dot_tn(own, h_ref[k]) + dot_tn(mate, h_mate_ref[k])
        out_ref[:UNIT, k * ff : (k + 1) * ff] = part.astype(BF)
    down = (dot_tn(dy_ref[...], gp_ref[...]) + dot_tn(dy_mate_ref[...], gp_mate_ref[...])).astype(BF)
    out_ref[UNIT:, :ff] = down[:EXTRA]
    out_ref[UNIT:, ff:] = down[EXTRA:]


def units_kernel(me_ref, *refs):
    del me_ref
    own, mate, dy_a, dy_a_mate, dy_b, dy_b_mate = refs[:6]
    hid, outs = refs[6:10], refs[10:]
    for k, out in enumerate(outs):

        @pl.when(pl.program_id(0) == k)
        def _():
            dy = (dy_a, dy_a_mate) if k % 2 == 0 else (dy_b, dy_b_mate)
            unit_part(own, mate, *dy, *hid, out)


def units(me, first, mate_first, second, mate_second, h, h_mate, gp, gp_mate, hop, hops):
    _, slots, ff = h.shape
    at = lambda i, me: 2 * chip_at(me[0], hop + i // 2, i % 2 == 0) + me[0] % 2
    rows = pl.BlockSpec((slots, UNIT), lambda i, me: (0, 2 * at(i, me) + i % 2))
    grads_a = pl.BlockSpec((slots, PART_A), lambda i, me: (0, GRADS // PART_A + at(i - i % 2, me)))
    grads_b = pl.BlockSpec((slots, PART_B), lambda i, me: (0, at(i - i % 2 + 1, me)))
    shape = (UNIT + EXTRA, 2 * ff)
    free = (lambda x: x) if hop == 0 else in_hbm
    return pl.pallas_call(
        units_kernel,
        grid_spec=pltpu.PrefetchScalarGridSpec(
            num_scalar_prefetch=1,
            grid=(2 * hops,),
            in_specs=[rows, rows, grads_a, grads_a, grads_b, grads_b]
            + [held((2, slots, ff))] * 2
            + [held((slots, ff))] * 2,
            out_specs=[pl.BlockSpec(shape, lambda i, me: (0, 0))] * (2 * hops),
        ),
        out_shape=[pltpu.HBM(shape, BF)] * (2 * hops),
        compiler_params=params(30),
        name="units",
        cost_estimate=pl.CostEstimate(flops=4000000000, transcendentals=0, bytes_accessed=12000000),
    )(
        me,
        *map(in_hbm, (first, mate_first, first, mate_first)),
        *map(free, (second, mate_second)),
        in_hbm(h),
        free(h_mate),
        in_hbm(gp),
        free(gp_mate),
    )


def unpack_kernel(hot_ref, rows_ref, ids_ref, gates_ref, out_ref, gate_ref):
    out_ref[...] = dot_tn(hot_ref[...], rows_ref[...]).astype(BF)

    @pl.when(pl.program_id(0) == 0)
    def _():
        hot = hot_ref[...]
        expert = lax.broadcasted_iota(jnp.int32, hot.shape, 0) // CAP
        for k in range(2):
            chosen = jnp.where(expert == ids_ref[k : k + 1, :], hot.astype(F32), 0.0).astype(BF)
            gate_ref[k : k + 1, :] = dot_tn(gates_ref[...], chosen)[0:1, :].astype(BF)


def unpack(hot, ids, back, width):
    slots, tok_dev = hot.shape
    blk = 1024
    whole = lambda shape: pl.BlockSpec(shape, lambda i: (0, 0))
    return pl.pallas_call(
        unpack_kernel,
        grid=(width // blk,),
        in_specs=[
            whole((slots, tok_dev)),
            pl.BlockSpec((slots, blk), lambda i: (0, i)),
            whole((2, tok_dev)),
            pl.BlockSpec((slots, LANES), lambda i: (0, width // LANES)),
        ],
        out_specs=[pl.BlockSpec((tok_dev, blk), lambda i: (0, i)), whole((2, tok_dev))],
        out_shape=[pltpu.HBM((tok_dev, width), BF), pltpu.HBM((2, tok_dev), BF)],
        compiler_params=params(16),
        name="unpack",
        cost_estimate=pl.CostEstimate(flops=1000000000, transcendentals=0, bytes_accessed=10000000),
    )(*map(in_hbm, (hot, back, ids, back)))


SWAP = [(i, i ^ 1) for i in range(8)]
UP = [(i, (i + 2) % 8) for i in range(8)]
DOWN = [(i, (i - 2) % 8) for i in range(8)]


def pass_on(up, dn):
    return lax.ppermute(up, "dp", UP), lax.ppermute(dn, "dp", DOWN)


def added(arrived, parts):
    return tuple((a.astype(F32) + b.astype(F32)).astype(BF) for a, b in zip(arrived, parts))


def body(tokens_in, out_grad, expert_ids, gate_probs, gate_up, down_proj):
    width = tokens_in.shape[1]
    owners = lax.axis_size("expert")
    ff = gate_up.shape[3]
    slots = owners * CAP
    me = lax.axis_index("dp")

    ids = expert_ids.T
    first, second, hot = pack(ids, gate_probs.T, tokens_in, out_grad, slots)

    def exchange(rows):
        wide = rows.shape[1]
        got = lax.all_to_all(rows.reshape(owners, CAP, wide), "expert", split_axis=0, concat_axis=0, tiled=True)
        return got.reshape(slots, wide)

    def swap(x):
        return lax.ppermute(x, "dp", SWAP)

    me = me.reshape(1).astype(jnp.int32)
    first, me = lax.optimization_barrier((first, me))
    first, gate_up, down_proj = lax.optimization_barrier((exchange(first), gate_up, down_proj))
    second = exchange(second)
    mate_first = swap(first)
    w = jnp.transpose(gate_up[:, :, 0], (1, 0, 2))
    wd = down_proj.reshape(SLICES, 2, PART_A, ff)
    u_a, c1, c2, p, gp = pre(first, w, wd)
    gp_mate = swap(gp)
    second, gp_mate = lax.optimization_barrier((second, gp_mate))
    mate_second = swap(second)
    h, rows = hidden(second, wd, u_a, c1, c2, p, width)
    h_mate = swap(h)
    args = (me, first, mate_first, second, mate_second)
    total = units(*args, h, h_mate, gp, gp_mate, 0, 1)
    h, total = lax.optimization_barrier((h, total))
    total = pass_on(*total)
    rows = input_rows(h, w, 0, width, rows)
    h, rows = lax.optimization_barrier((h, rows))
    back = exchange(rows)
    parts = units(*args, h, h_mate, gp, gp_mate, 1, 1)
    total = added(total, parts)
    h, total = lax.optimization_barrier((h, total))
    total = pass_on(*total)
    parts = units(*args, h, h_mate, gp, gp_mate, 2, 2)
    total = pass_on(*added(total, parts[:2]))
    input_grad, gate_grad = unpack(hot, ids, back, width)
    total, input_grad = lax.optimization_barrier((total, input_grad))
    sum_up, sum_dn = added(total, parts[2:])

    sums = jnp.concatenate([sum_up[:UNIT], sum_dn[:UNIT]], axis=0)
    gate_up_grad = sums.reshape(SLICE, 2, 1, ff)
    down = [t[UNIT:, k * ff : (k + 1) * ff] for t in (sum_up, sum_dn) for k in range(2)]
    down_grad = jnp.concatenate(down, axis=0)[:, None, :]
    return (input_grad, gate_grad.T, gate_up_grad, down_grad)


def solution(mesh):
    placed = (
        P(("dp", "expert"), None),
        P(("dp", "expert"), None),
        P(("dp", "expert"), None),
        P(("dp", "expert"), None),
        P(None, None, "expert", None),
        P(None, "expert", None),
    )
    return jax.shard_map(
        body,
        mesh=mesh,
        in_specs=placed,
        out_specs=(
            P(("dp", "expert"), None),
            P(("dp", "expert"), None),
            P("dp", None, "expert", None),
            P("dp", "expert", None),
        ),
        check_vma=False,
    )
```

```python
import functools

import jax
import jax.numpy as jnp
from jax import lax
from jax.experimental import pallas as pl
from jax.experimental.pallas import tpu as pltpu
from jax.sharding import PartitionSpec as P

BF = jnp.bfloat16
F32 = jnp.float32
SLICE = 512
PART_A = 256
PART_B = SLICE - PART_A
SLICES = 8
GRADS = SLICES * SLICE
FIRST = GRADS + SLICES * PART_A
CAP = 32
LANES = 128
PACK_STEPS = 2
PRE_PER = 2
INPUT_BLOCK = 2048


def params(mib):
    return pltpu.CompilerParams(vmem_limit_bytes=mib * 1024 * 1024)


def in_hbm(x):
    return pltpu.with_memory_space_constraint(x, pltpu.HBM)


def in_vmem(x):
    return pltpu.with_memory_space_constraint(x, pltpu.VMEM)


def held(shape):
    return pl.BlockSpec(shape, lambda *_: (0,) * len(shape), pipeline_mode=pl.Buffered(1))


def left_in_hbm():
    return pl.BlockSpec(memory_space=pltpu.HBM)


def dot_nn(a, b):
    return lax.dot_general(a, b, (((1,), (0,)), ((), ())), preferred_element_type=F32)


def dot_nt(a, b):
    return lax.dot_general(a, b, (((1,), (1,)), ((), ())), preferred_element_type=F32)


def dot_tn(a, b):
    return lax.dot_general(a, b, (((0,), (0,)), ((), ())), preferred_element_type=F32)


def pack_kernel(ids_ref, gates_ref, tok_ref, dy_ref, first_ref, second_ref, hot_ref, *, step_experts):
    tokens = ids_ref.shape[1]
    base = pl.program_id(0) * step_experts
    expert = lax.broadcasted_iota(jnp.int32, (8, tokens), 0) + base
    zero = jnp.zeros((8, tokens), F32)
    is_0 = ids_ref[0:1, :] == expert
    is_1 = ids_ref[1:2, :] == expert
    named = is_0 | is_1
    member = jnp.where(named, 1.0, 0.0).astype(BF)
    row = lax.broadcasted_iota(jnp.int32, (tokens, tokens), 0)
    col = lax.broadcasted_iota(jnp.int32, (tokens, tokens), 1)
    earlier = jnp.where(row < col, 1.0, 0.0).astype(BF)
    place = jnp.where(named, dot_nn(member, earlier), -1.0)
    gates = gates_ref[...].astype(F32)
    weight = jnp.where(is_0, gates[0:1, :], zero) + jnp.where(is_1, gates[1:2, :], zero)
    rows = step_experts * CAP
    place_all = jnp.broadcast_to(place[:step_experts, None, :], (step_experts, CAP, tokens)).reshape(rows, tokens)
    weight_all = jnp.broadcast_to(weight[:step_experts, None, :], (step_experts, CAP, tokens)).reshape(rows, tokens)
    slot = (lax.broadcasted_iota(jnp.int32, (rows, tokens), 0) % CAP).astype(F32)
    hot = jnp.where(place_all == slot, 1.0, 0.0)
    slot_gate = jnp.sum(hot * weight_all, axis=1, keepdims=True)
    first_ref[:, FIRST:] = jnp.broadcast_to(slot_gate, (rows, LANES)).astype(BF)
    hot = hot.astype(BF)
    hot_ref[...] = hot
    for q in range(SLICES):
        cols = slice(q * SLICE, (q + 1) * SLICE)
        first_ref[:, cols] = dot_nn(hot, tok_ref[:, cols]).astype(BF)
        grads = dot_nn(hot, dy_ref[:, cols]).astype(BF)
        first_ref[:, GRADS + q * PART_A : GRADS + (q + 1) * PART_A] = grads[:, :PART_A]
        second_ref[:, q * PART_B : (q + 1) * PART_B] = grads[:, PART_A:]


def pack(ids, gates, tokens_in, out_grad, slots):
    steps = PACK_STEPS
    tok_dev, width = tokens_in.shape
    rows = slots // steps
    wide = FIRST + LANES
    whole = lambda shape: pl.BlockSpec(shape, lambda i: (0, 0))
    return pl.pallas_call(
        functools.partial(pack_kernel, step_experts=rows // CAP),
        grid=(steps,),
        in_specs=[whole((2, tok_dev)), whole((2, tok_dev)), whole((tok_dev, width)), whole((tok_dev, width))],
        out_specs=[
            pl.BlockSpec((rows, wide), lambda i: (i, 0)),
            pl.BlockSpec((rows, SLICES * PART_B), lambda i: (i, 0)),
            pl.BlockSpec((rows, tok_dev), lambda i: (i, 0)),
        ],
        out_shape=[
            pltpu.HBM((slots, wide), BF),
            pltpu.HBM((slots, SLICES * PART_B), BF),
            pltpu.HBM((slots, tok_dev), BF),
        ],
        compiler_params=params(24),
        name="pack",
        cost_estimate=pl.CostEstimate(flops=3000000000, transcendentals=0, bytes_accessed=14000000),
    )(in_hbm(ids), in_hbm(gates), in_hbm(tokens_in), in_hbm(out_grad))


def pre_kernel(rows_ref, dy_ref, gate_ref, w_ref, wd_ref, *refs, per):
    outs, (u_acc, pg_acc, pu_acc, p_buf, gp_buf, sems) = refs[:5], refs[5:]
    step = pl.program_id(0)

    @pl.when(step == 0)
    def _():
        pg_acc[...] = jnp.zeros_like(pg_acc)
        pu_acc[...] = jnp.zeros_like(pu_acc)
        u_acc[...] = jnp.zeros_like(u_acc)

    depth = pl.ds(pl.multiple_of(step * per * SLICE, SLICE), per * SLICE)
    u_acc[...] += dot_nn(dy_ref[...], wd_ref[...].reshape(per * PART_A, wd_ref.shape[3]))
    x = rows_ref[...]
    pg_acc[...] += dot_nn(x, w_ref[0, depth, :])
    pu_acc[...] += dot_nn(x, w_ref[1, depth, :])

    @pl.when(step == pl.num_programs(0) - 1)
    def _():
        slots = pg_acc.shape[0]
        chunk, part = 32, slots // 4
        copies = [pltpu.make_async_copy(u_acc, outs[0], sems.at[4, 0])]
        copies[0].start()
        for k in range(4):

            def one(i, carry):
                at = pl.ds(pl.multiple_of(k * part + i * chunk, chunk), chunk)
                pg = pg_acc[at, :]
                pu = pu_acc[at, :]
                g = gate_ref[at, :].astype(F32)[:, :1]
                s = jax.nn.sigmoid(pg)
                a = pg * s
                product = a * pu
                p_buf[at, :] = product.astype(BF)
                gp_buf[at, :] = (g * product).astype(BF)
                pg_acc[at, :] = g * (pu * s * (1.0 + pg * (1.0 - s)))
                pu_acc[at, :] = g * a
                return carry

            lax.fori_loop(0, part // chunk, one, 0)
            for j, (buf, out) in enumerate(zip((pg_acc, pu_acc, p_buf, gp_buf), outs[1:])):
                at = pl.ds(k * part, part)
                copies.append(pltpu.make_async_copy(buf.at[at], out.at[at], sems.at[j, k]))
                copies[-1].start()
        for copy in copies:
            copy.wait()


def pre(first, w, wd):
    slots = first.shape[0]
    ff = wd.shape[3]
    per = PRE_PER
    return pl.pallas_call(
        functools.partial(pre_kernel, per=per),
        grid=(SLICES // per,),
        in_specs=[
            pl.BlockSpec((slots, per * SLICE), lambda q: (0, q)),
            pl.BlockSpec((slots, per * PART_A), lambda q: (0, GRADS // (per * PART_A) + q)),
            pl.BlockSpec((slots, LANES), lambda q: (0, FIRST // LANES)),
            pl.BlockSpec(memory_space=pltpu.VMEM),
            pl.BlockSpec((per, 1, PART_A, ff), lambda q: (q, 0, 0, 0)),
        ],
        out_specs=[left_in_hbm()] * 5,
        out_shape=[pltpu.HBM((slots, ff), t) for t in (F32, F32, F32, BF, BF)],
        scratch_shapes=[pltpu.VMEM((slots, ff), t) for t in (F32, F32, F32, BF, BF)]
        + [pltpu.SemaphoreType.DMA((5, 4))],
        compiler_params=params(24),
        name="pre",
        cost_estimate=pl.CostEstimate(flops=17000000000, transcendentals=0, bytes_accessed=40000000),
    )(in_hbm(first), in_hbm(first), in_hbm(first), in_vmem(w), in_hbm(wd))


def hidden_kernel(dy_hbm, wd_hbm, u_hbm, c1_hbm, c2_hbm, p_hbm, h_ref, gate_ref, *scratch):
    dy, wd, u_acc, c1, c2, p, gate_acc, sems = scratch
    half = SLICES // 2
    depth = half * PART_B
    wanted = [
        (dy_hbm, dy),
        (wd_hbm.at[:half, 1], wd.at[:half]),
        (wd_hbm.at[half:, 1], wd.at[half:]),
        (u_hbm, u_acc),
        (c1_hbm, c1),
        (c2_hbm, c2),
        (p_hbm, p),
    ]
    copies = [pltpu.make_async_copy(src, dst, sems.at[k]) for k, (src, dst) in enumerate(wanted)]
    for copy in copies:
        copy.start()
    copies[0].wait()
    copies[1].wait()
    copies[3].wait()
    u_acc[...] += dot_nn(dy[:, :depth], wd[:half].reshape(depth, wd.shape[2]))
    copies[2].wait()
    u_acc[...] += dot_nn(dy[:, depth:], wd[half:].reshape(depth, wd.shape[2]))
    for copy in copies[4:]:
        copy.wait()
    chunk = 64

    def one(i, carry):
        at = pl.ds(pl.multiple_of(i * chunk, chunk), chunk)
        u = u_acc[at, :]
        h_ref[0, at, :] = (u * c1[at, :]).astype(BF)
        h_ref[1, at, :] = (u * c2[at, :]).astype(BF)
        both = u * p[at, :].astype(F32)
        folded = both[:, :LANES]
        for k in range(1, both.shape[1] // LANES):
            folded += both[:, k * LANES : (k + 1) * LANES]
        gate_acc[at, :] = folded
        return carry

    lax.fori_loop(0, u_acc.shape[0] // chunk, one, 0)
    total = jnp.sum(gate_acc[...], axis=1, keepdims=True)
    gate_ref[...] = jnp.broadcast_to(total, gate_ref.shape).astype(BF)


def hidden(second, wd, u_a, c1, c2, p, gate_at):
    slots, ff = p.shape
    return pl.pallas_call(
        hidden_kernel,
        grid=(1,),
        in_specs=[pl.BlockSpec(memory_space=pl.ANY)] + [left_in_hbm()] * 5,
        out_specs=[held((2, slots, ff)), pl.BlockSpec((slots, LANES), lambda j: (0, gate_at // LANES))],
        out_shape=[pltpu.HBM((2, slots, ff), BF), pltpu.HBM((slots, gate_at + LANES), BF)],
        scratch_shapes=[
            pltpu.VMEM(second.shape, BF),
            pltpu.VMEM((SLICES, PART_B, ff), BF),
            pltpu.VMEM((slots, ff), F32),
            pltpu.VMEM((slots, ff), F32),
            pltpu.VMEM((slots, ff), F32),
            pltpu.VMEM((slots, ff), BF),
            pltpu.VMEM((slots, LANES), F32),
            pltpu.SemaphoreType.DMA((7,)),
        ],
        compiler_params=params(24),
        name="hidden",
        cost_estimate=pl.CostEstimate(flops=4000000000, transcendentals=0, bytes_accessed=14000000),
    )(second, *map(in_hbm, (wd, u_a, c1, c2, p)))


def input_kernel(h_ref, w_ref, into_ref, out_ref):
    del into_ref
    out_ref[...] = (dot_nt(h_ref[0], w_ref[0]) + dot_nt(h_ref[1], w_ref[1])).astype(BF)


def input_rows(h, w, begin, cols, into):
    _, slots, ff = h.shape
    blk = INPUT_BLOCK
    first = begin // blk
    return pl.pallas_call(
        input_kernel,
        grid=(cols // blk,),
        in_specs=[held((2, slots, ff)), pl.BlockSpec((2, blk, ff), lambda j: (0, first + j, 0)), left_in_hbm()],
        out_specs=pl.BlockSpec((slots, blk), lambda j: (0, first + j)),
        out_shape=pltpu.HBM(into.shape, BF),
        input_output_aliases={2: 0},
        compiler_params=params(24),
        name="input_rows",
        cost_estimate=pl.CostEstimate(flops=13000000000, transcendentals=0, bytes_accessed=24000000),
    )(in_hbm(h), in_hbm(w), in_hbm(into))


def chip_at(me, hop, up):
    return jnp.where(up, me // 2 + 3 - hop, me // 2 + 1 + hop) % 4


UNIT = SLICE // 2
EXTRA = UNIT // 2


def unit_part(own_ref, mate_ref, dy_ref, dy_mate_ref, h_ref, h_mate_ref, gp_ref, gp_mate_ref, out_ref):
    ff = gp_ref.shape[1]
    own = own_ref[...]
    mate = mate_ref[...]
    for k in range(2):
        part = dot_tn(own, h_ref[k]) + dot_tn(mate, h_mate_ref[k])
        out_ref[:UNIT, k * ff : (k + 1) * ff] = part.astype(BF)
    down = (dot_tn(dy_ref[...], gp_ref[...]) + dot_tn(dy_mate_ref[...], gp_mate_ref[...])).astype(BF)
    out_ref[UNIT:, :ff] = down[:EXTRA]
    out_ref[UNIT:, ff:] = down[EXTRA:]


def units_kernel(me_ref, *refs):
    del me_ref
    own, mate, dy_a, dy_a_mate, dy_b, dy_b_mate = refs[:6]
    hid, outs = refs[6:10], refs[10:]
    for k, out in enumerate(outs):

        @pl.when(pl.program_id(0) == k)
        def _():
            dy = (dy_a, dy_a_mate) if k % 2 == 0 else (dy_b, dy_b_mate)
            unit_part(own, mate, *dy, *hid, out)


def units(me, first, mate_first, second, mate_second, h, h_mate, gp, gp_mate, hop, hops):
    _, slots, ff = h.shape
    at = lambda i, me: 2 * chip_at(me[0], hop + i // 2, i % 2 == 0) + me[0] % 2
    rows = pl.BlockSpec((slots, UNIT), lambda i, me: (0, 2 * at(i, me) + i % 2))
    grads_a = pl.BlockSpec((slots, PART_A), lambda i, me: (0, GRADS // PART_A + at(i - i % 2, me)))
    grads_b = pl.BlockSpec((slots, PART_B), lambda i, me: (0, at(i - i % 2 + 1, me)))
    shape = (UNIT + EXTRA, 2 * ff)
    free = (lambda x: x) if hop == 0 else in_hbm
    return pl.pallas_call(
        units_kernel,
        grid_spec=pltpu.PrefetchScalarGridSpec(
            num_scalar_prefetch=1,
            grid=(2 * hops,),
            in_specs=[rows, rows, grads_a, grads_a, grads_b, grads_b]
            + [held((2, slots, ff))] * 2
            + [held((slots, ff))] * 2,
            out_specs=[pl.BlockSpec(shape, lambda i, me: (0, 0))] * (2 * hops),
        ),
        out_shape=[pltpu.HBM(shape, BF)] * (2 * hops),
        compiler_params=params(30),
        name="units",
        cost_estimate=pl.CostEstimate(flops=4000000000, transcendentals=0, bytes_accessed=12000000),
    )(
        me,
        *map(in_hbm, (first, mate_first, first, mate_first)),
        *map(free, (second, mate_second)),
        in_hbm(h),
        free(h_mate),
        in_hbm(gp),
        free(gp_mate),
    )


def unpack_kernel(hot_ref, rows_ref, ids_ref, gates_ref, out_ref, gate_ref):
    out_ref[...] = dot_tn(hot_ref[...], rows_ref[...]).astype(BF)

    @pl.when(pl.program_id(0) == 0)
    def _():
        hot = hot_ref[...]
        expert = lax.broadcasted_iota(jnp.int32, hot.shape, 0) // CAP
        for k in range(2):
            chosen = jnp.where(expert == ids_ref[k : k + 1, :], hot.astype(F32), 0.0).astype(BF)
            gate_ref[k : k + 1, :] = dot_tn(gates_ref[...], chosen)[0:1, :].astype(BF)


def unpack(hot, ids, back, width):
    slots, tok_dev = hot.shape
    blk = 1024
    whole = lambda shape: pl.BlockSpec(shape, lambda i: (0, 0))
    return pl.pallas_call(
        unpack_kernel,
        grid=(width // blk,),
        in_specs=[
            whole((slots, tok_dev)),
            pl.BlockSpec((slots, blk), lambda i: (0, i)),
            whole((2, tok_dev)),
            pl.BlockSpec((slots, LANES), lambda i: (0, width // LANES)),
        ],
        out_specs=[pl.BlockSpec((tok_dev, blk), lambda i: (0, i)), whole((2, tok_dev))],
        out_shape=[pltpu.HBM((tok_dev, width), BF), pltpu.HBM((2, tok_dev), BF)],
        compiler_params=params(16),
        name="unpack",
        cost_estimate=pl.CostEstimate(flops=1000000000, transcendentals=0, bytes_accessed=10000000),
    )(*map(in_hbm, (hot, back, ids, back)))


SWAP = [(i, i ^ 1) for i in range(8)]
UP = [(i, (i + 2) % 8) for i in range(8)]
DOWN = [(i, (i - 2) % 8) for i in range(8)]


def pass_on(up, dn):
    return lax.ppermute(up, "dp", UP), lax.ppermute(dn, "dp", DOWN)


def added(arrived, parts):
    return tuple((a.astype(F32) + b.astype(F32)).astype(BF) for a, b in zip(arrived, parts))


def body(tokens_in, out_grad, expert_ids, gate_probs, gate_up, down_proj):
    width = tokens_in.shape[1]
    owners = lax.axis_size("expert")
    ff = gate_up.shape[3]
    slots = owners * CAP
    me = lax.axis_index("dp")

    ids = expert_ids.T
    first, second, hot = pack(ids, gate_probs.T, tokens_in, out_grad, slots)

    def exchange(rows):
        wide = rows.shape[1]
        got = lax.all_to_all(rows.reshape(owners, CAP, wide), "expert", split_axis=0, concat_axis=0, tiled=True)
        return got.reshape(slots, wide)

    def swap(x):
        return lax.ppermute(x, "dp", SWAP)

    me = me.reshape(1).astype(jnp.int32)
    first, me = lax.optimization_barrier((first, me))
    first, gate_up, down_proj = lax.optimization_barrier((exchange(first), gate_up, down_proj))
    second = exchange(second)
    mate_first = swap(first)
    w = jnp.transpose(gate_up[:, :, 0], (1, 0, 2))
    wd = down_proj.reshape(SLICES, 2, PART_A, ff)
    u_a, c1, c2, p, gp = pre(first, w, wd)
    gp_mate = swap(gp)
    second, gp_mate = lax.optimization_barrier((second, gp_mate))
    mate_second = swap(second)
    h, rows = hidden(second, wd, u_a, c1, c2, p, width)
    h_mate = swap(h)
    args = (me, first, mate_first, second, mate_second)
    total = units(*args, h, h_mate, gp, gp_mate, 0, 1)
    h, total = lax.optimization_barrier((h, total))
    total = pass_on(*total)
    rows = input_rows(h, w, 0, width, rows)
    h, rows = lax.optimization_barrier((h, rows))
    back = exchange(rows)
    parts = units(*args, h, h_mate, gp, gp_mate, 1, 1)
    total = added(total, parts)
    h, total = lax.optimization_barrier((h, total))
    total = pass_on(*total)
    parts = units(*args, h, h_mate, gp, gp_mate, 2, 2)
    total = pass_on(*added(total, parts[:2]))
    input_grad, gate_grad = unpack(hot, ids, back, width)
    total, input_grad = lax.optimization_barrier((total, input_grad))
    sum_up, sum_dn = added(total, parts[2:])

    sums = jnp.concatenate([sum_up[:UNIT], sum_dn[:UNIT]], axis=0)
    gate_up_grad = sums.reshape(SLICE, 2, 1, ff)
    down = [t[UNIT:, k * ff : (k + 1) * ff] for t in (sum_up, sum_dn) for k in range(2)]
    down_grad = jnp.concatenate(down, axis=0)[:, None, :]
    return (input_grad, gate_grad.T, gate_up_grad, down_grad)


def solution(mesh):
    placed = (
        P(("dp", "expert"), None),
        P(("dp", "expert"), None),
        P(("dp", "expert"), None),
        P(("dp", "expert"), None),
        P(None, None, "expert", None),
        P(None, "expert", None),
    )
    return jax.shard_map(
        body,
        mesh=mesh,
        in_specs=placed,
        out_specs=(
            P(("dp", "expert"), None),
            P(("dp", "expert"), None),
            P("dp", None, "expert", None),
            P("dp", "expert", None),
        ),
        check_vma=False,
    )
```
